512 devices in a mesh: ctx: 64 (over x, z_lo, y), tp: 8 (over z_hi, core).
Axes of the slice: x: 4, y: 8, z: 8 (z_hi: 4, z_lo: 2; z = z_hi * 2 + z_lo), core: 2. Of those that a mesh axis runs over, the one named last changes fastest.
Arguments:
- queries: bfloat16 [49152, 2048], P('ctx', 'tp'), may hold values from -9 to 9
- keys: bfloat16 [49152, 2048], P('ctx', 'tp'), may hold values from -130 to 130
- values: bfloat16 [49152, 2048], P('ctx', 'tp'), may hold values from -6 to 6
- residual: bfloat16 [49152, 3072], P('ctx', 'tp'), may hold values from -3 to 3
- gate: float32 [3072], P('tp'), may hold values from 1 to 4
- out_weight: bfloat16 [2048, 3072], P('tp'), may hold values from -0.1875 to 0.1875
Outputs:
- mixed: bfloat16 [49152, 3072], P('ctx', 'tp')
The draws below stay inside these ranges and needn't reach their ends.
All inputs are finite; a program needn't handle non-finite values.
Results may differ from the reference program's by a relative error of at most 0.014.
Values may be sent and summed in bfloat16 or wider, within the bound.
A program may use at most 64 MiB of HBM per device.

```python
import jax
import jax.numpy as jnp
from jax import lax

D = 3072
HEADS = 16
HEAD_DIM = 128
TOK_DEV = 768
CYCLE = 8
SEQS = 8
TOKENS = 49152
N_TP = 8


def joint_draw(key):
    width_all = HEADS * HEAD_DIM
    query_full = jnp.clip(1.5 * jax.random.normal(jax.random.fold_in(key, 11), (TOKENS, width_all), jnp.float32), -9.0, 9.0)
    key_full = jnp.clip(1.5 * jax.random.normal(jax.random.fold_in(key, 12), (TOKENS, width_all), jnp.float32), -9.0, 9.0)
    return (query_full, key_full)


def draw_queries(key, part):
    return joint_draw(key)[0].astype(jnp.bfloat16)


def draw_keys(key, part):
    return joint_draw(key)[1].astype(jnp.bfloat16)


def with_spikes(drawn, own_key, source, target, parts, factor):
    def block_of(dim):
        return (jnp.arange(drawn.shape[dim]) // (drawn.shape[dim] // parts)).reshape((-1,) + (1,) * (drawn.ndim - 1 - dim))

    near = jax.random.permutation(own_key, parts)[block_of(target)]
    second = (block_of(target) + parts // 2) % parts
    return jnp.where((block_of(source) == near) | (block_of(source) == second), factor * drawn, drawn)


def block_levels(key, dims, shards, least, largest):
    def one(position, blocks):
        heights = jax.random.uniform(jax.random.fold_in(jax.random.fold_in(key, 6), position), (blocks,), jnp.float32, least / len(shards), largest / len(shards))
        return jnp.repeat(jnp.exp(heights), dims[position] // blocks).reshape((-1,) + (1,) * (len(dims) - position - 1))

    gain = one(*shards[0])
    for cut in shards[1:]:
        gain = gain * one(*cut)
    return gain


def bell_draw(rng, dims, width, limit, cuts=(), held_as=jnp.bfloat16):
    level = block_levels(rng, dims, cuts, -0.22, 0.18) if cuts else 1.0
    values = jax.random.normal(rng, dims, jnp.float32) * width * level
    return jnp.minimum(jnp.maximum(values, -limit), limit).astype(held_as)


def heavy_noise(key, shape, deviation, most, split, heavy, held_as=jnp.bfloat16):
    values = deviation * jax.random.normal(key, shape, jnp.float32)
    if split:
        values = values * block_levels(key, shape, split, -0.22, 0.18)
    return jnp.clip(with_spikes(values, jax.random.fold_in(key, 3), *heavy), -most, most).astype(held_as)


def setup_inputs(seed: int = 0) -> dict:
    key_list = jax.random.split(jax.random.key(seed), 7)
    queries = draw_queries(jax.random.fold_in(key_list[6], 71), 0)
    keys = draw_keys(jax.random.fold_in(key_list[6], 71), 0)
    values = bell_draw(key_list[2], (TOKENS, HEADS * HEAD_DIM), 1.0, 6.0, ((0, 64), (1, 8)))
    residual = bell_draw(key_list[3], (TOKENS, D), 0.5, 3.0, ((0, 64), (1, 8)))
    gate = jnp.clip(1.0 + 3.0 * jax.random.uniform(key_list[4], (D,), jnp.float32) ** block_levels(key_list[4], (D,), ((0, 8),), -0.2, 0.2), 1.0, 4.0)
    out_weight = heavy_noise(key_list[5], (HEADS * HEAD_DIM, D), (HEADS * HEAD_DIM) ** -0.5, 0.1875, ((0, 8),), (0, 1, 8, 2.0))
    return {"queries": queries, "keys": keys, "values": values, "residual": residual, "gate": gate, "out_weight": out_weight}


def arrange(array):
    shaped = array.reshape(CYCLE, SEQS, TOK_DEV, HEADS, HEAD_DIM)
    return shaped.transpose(1, 0, 2, 3, 4).reshape(SEQS, CYCLE * TOK_DEV, HEADS, HEAD_DIM)


def reference(queries, keys, values, residual, gate, out_weight):
    length = CYCLE * TOK_DEV
    width_all = HEADS * HEAD_DIM
    scale = 1.0 / (HEAD_DIM ** 0.5)
    query_seq = arrange(queries)
    key_seq = arrange(keys)
    value_seq = arrange(values)
    block = min(512, length)
    blocks = length // block

    def one_block(index):
        seq_index = index // blocks
        block_index = index % blocks
        query_all = lax.dynamic_index_in_dim(query_seq, seq_index, 0, keepdims=False)
        query_block = lax.dynamic_slice_in_dim(query_all, (block_index * block).astype(jnp.int32), block, 0)
        key_all = lax.dynamic_index_in_dim(key_seq, seq_index, 0, keepdims=False)
        value_all = lax.dynamic_index_in_dim(value_seq, seq_index, 0, keepdims=False)
        scores = jnp.einsum("qhd,khd->hqk", query_block.astype(jnp.float32), key_all.astype(jnp.float32)) * scale
        top = jnp.max(scores, axis=-1, keepdims=True)
        weights = jnp.exp(scores - top)
        total = jnp.sum(weights, axis=-1)
        rounded = lax.optimization_barrier(weights.astype(jnp.bfloat16)).astype(jnp.float32)
        summed = jnp.einsum("hqk,khd->qhd", rounded, value_all.astype(jnp.float32))
        return (summed / total.T[:, :, None]).astype(jnp.bfloat16)

    result = lax.map(one_block, jnp.arange(SEQS * blocks, dtype=jnp.int32))
    result = result.reshape(SEQS, CYCLE, TOK_DEV, HEADS, HEAD_DIM).transpose(1, 0, 2, 3, 4)
    attended = result.reshape(TOKENS, width_all)
    group = width_all // N_TP

    def add_group(counter, accum):
        start = (counter * group).astype(jnp.int32)
        columns = lax.dynamic_slice_in_dim(attended, start, group, 1)
        rows = lax.dynamic_slice_in_dim(out_weight, start, group, 0)
        partial_value = jnp.dot(columns, rows, preferred_element_type=jnp.float32)
        return accum + lax.optimization_barrier(partial_value.astype(jnp.bfloat16)).astype(jnp.float32)

    projected = lax.fori_loop(0, N_TP, add_group, jnp.zeros((TOKENS, D), jnp.float32))
    return (residual.astype(jnp.float32) + gate[None, :] * projected).astype(jnp.bfloat16)
```

```python
import functools
import math

import jax
import jax.numpy as jnp
from jax import lax
from jax.experimental import pallas as pl
from jax.experimental.pallas import tpu as pltpu
from jax.sharding import PartitionSpec as P

MESH = pl.DeviceIdType.MESH
HD = 128
NX, NZL, NY, NZH = 4, 2, 8, 4
TOK = 768
HALF = TOK // 2
FEAT = 768
FC = FEAT // 2
SCALE = math.log2(math.e) / math.sqrt(HD)
BF = jnp.bfloat16
F32 = jnp.float32

R_A, R_B, R_Z, R_Q = 0, 4, 12, 16
R_RET, R_G3, R_G1, R_H = 20, 24, 28, 32
R_WZ, R_WX, R_WY, R_WP, R_WO, R_WL = 40, 44, 48, 56, 57, 58
R_RES, R_GATE, R_RL, R_GL, R_OUT, R_OL = 59, 60, 61, 62, 63, 64
N_RECV = 65


def kernel(q_ref, k_ref, v_ref, res_ref, gate_ref, w_ref, out_ref,
           qb, kv, att, ob, wb, resb, gateb, mst, acc, oacc, mixb, ss, rs):
    ctx = lax.axis_index("ctx")
    tp = lax.axis_index("tp")
    x, zl, y = ctx // (NZL * NY), (ctx // NY) % NZL, ctx % NY
    zh, c = tp // 2, tp % 2

    def dev(dx=0, dzl=0, dy=0, dzh=0, dc=0):
        return ((((x + dx) % NX) * NZL + (zl + dzl) % NZL) * NY + (y + dy) % NY,
                ((zh + dzh) % NZH) * 2 + (c + dc) % 2)

    def dev_abs(xd, r):
        return ((xd * NZL + zl) * NY + y, zh * 2 + r)

    sends = []
    count = [0]

    def send(src, dst, device, recv):
        i = count[0]
        count[0] += 1
        copy = pltpu.make_async_remote_copy(
            src_ref=src, dst_ref=dst, send_sem=ss.at[i], recv_sem=rs.at[recv],
            device_id=device, device_id_type=MESH)
        copy.start()
        sends.append(copy)

    def local(src, dst, recv):
        pltpu.make_async_copy(src, dst, rs.at[recv]).start()

    def arrived(dst, recv):
        pltpu.make_async_copy(dst, dst, rs.at[recv]).wait()

    mine = pl.ds(pl.multiple_of(c * HALF, HALF), HALF)
    theirs = pl.ds(pl.multiple_of((1 - c) * HALF, HALF), HALF)
    wcols = pl.ds(pl.multiple_of(zh * FEAT, FEAT), FEAT)

    local(w_ref.at[:, wcols], wb.at[0, c], R_WL)
    local(res_ref.at[mine, :], resb.at[0], R_RL)
    local(gate_ref, gateb.at[0], R_GL)

    peers = [dev(dx=d, dc=e) for d in (1, 2, 3) for e in (0, 1)]
    peers += [dev(dc=1), dev(dzl=1)]
    peers += [dev(dzh=d) for d in (1, 2, 3)]
    peers += [dev(dy=d) for d in range(1, NY)]
    barrier = pltpu.get_barrier_semaphore()
    for peer in peers:
        pl.semaphore_signal(barrier, inc=1, device_id=peer, device_id_type=MESH)
    pl.semaphore_wait(barrier, len(peers))

    wrow = pl.ds(pl.multiple_of(y * 32 + (x % 2) * 16, 16), 16)
    wcol = (x // 2) * FC
    for d in (1, 2, 3):
        zd = (zh + d) % NZH
        send(w_ref.at[wrow, pl.ds(pl.multiple_of(zd * FEAT + wcol, FC), FC)],
             wb.at[4 - d, c, wrow, pl.ds(pl.multiple_of(wcol, FC), FC)],
             dev(dzh=d), R_WZ + 4 - d)

    first = jnp.where((2 * c - x) % NX == 2, 1, 0)
    waits = []
    for j in (0, 1):
        head = (j + first) % 2
        xd = 2 * c + head
        slot = (x - xd) % NX
        cols = pl.ds(pl.multiple_of(head * HD, HD), HD)
        for kind in ("kv", "q"):
            for r in (0, 1):
                rows = pl.ds(r * HALF, HALF)
                here = (xd == x) & (c == r)
                if kind == "kv":
                    parts = [(k_ref, kv.at[slot, 0, rows, :]), (v_ref, kv.at[slot, 1, rows, :])]
                    recv = R_A + slot
                else:
                    parts = [(q_ref, qb.at[slot])]
                    recv = R_Q + slot
                base = count[0]
                count[0] += len(parts)

                @pl.when(here)
                def _(parts=parts, rows=rows, cols=cols, recv=recv):
                    for src, dst in parts:
                        pltpu.make_async_copy(src.at[rows, cols], dst, rs.at[recv]).start()

                @pl.when(jnp.logical_not(here))
                def _(parts=parts, rows=rows, cols=cols, recv=recv, base=base, xd=xd, r=r):
                    for n, (src, dst) in enumerate(parts):
                        pltpu.make_async_remote_copy(
                            src_ref=src.at[rows, cols], dst_ref=dst, send_sem=ss.at[base + n],
                            recv_sem=rs.at[recv], device_id=dev_abs(xd, r),
                            device_id_type=MESH).start()

                waits.append((here, parts, rows, cols, base, recv, xd, r))

    def init(n, _):
        mst[n] = jnp.full((HALF, HD), -1e30, F32)
        acc[n] = jnp.zeros((HALF, 2 * HD), F32)
        return 0

    lax.fori_loop(0, NX, init, 0)

    def attend(i, s):
        k = kv[s, 0]
        v = jnp.concatenate([kv[s, 1], jnp.ones((TOK, HD), BF)], axis=1)
        tq = 192
        for t in range(HALF // tq):
            rows = pl.ds(t * tq, tq)
            sc = lax.dot_general(qb[i, rows, :], k, (((1,), (1,)), ((), ())),
                                 preferred_element_type=F32) * SCALE
            old = mst[i, rows, :]
            new = jnp.maximum(old, jnp.max(sc, axis=1, keepdims=True))
            p = jnp.exp2(sc - jnp.concatenate([new] * (TOK // HD), axis=1)).astype(BF)
            alpha = jnp.exp2(old - new)
            pv = jnp.dot(p, v, preferred_element_type=F32)
            acc[i, rows, :] = acc[i, rows, :] * jnp.concatenate([alpha, alpha], axis=1) + pv
            mst[i, rows, :] = new

    def items(pairs):
        if len(pairs) == 1:
            attend(*pairs[0])
            return
        icode = sum(i << (2 * n) for n, (i, _) in enumerate(pairs))
        scode = [sum(s << (3 * n) for n, (_, s) in enumerate(pairs[b:b + 10])) for b in (0, 10)]

        def body(n, _):
            i = (jnp.int32(icode) >> (2 * n)) & 3
            if len(pairs) <= 10:
                s = (jnp.int32(scode[0]) >> (3 * n)) & 7
            else:
                s = jnp.where(n < 10, jnp.int32(scode[0]) >> (3 * jnp.minimum(n, 9)),
                              jnp.int32(scode[1]) >> (3 * jnp.maximum(n - 10, 0))) & 7
            attend(i, s)
            return 0

        lax.fori_loop(0, len(pairs), body, 0)

    def half_of(s, rows):
        return kv.at[s, :, rows, :]

    def pass_own(d):
        arrived(half_of(d, mine), R_A + d)
        send(half_of(d, mine), half_of(d, mine), dev(dc=1), R_B + d)
        send(half_of(d, mine), half_of(4 + d, mine), dev(dzl=1), R_Z + d)

    def pass_other(d):
        arrived(half_of(4 + d, mine), R_Z + d)
        send(half_of(4 + d, mine), half_of(4 + d, mine), dev(dc=1), R_B + 4 + d)

    def whole(s):
        arrived(half_of(s, theirs), R_B + s)

    def queries(d):
        arrived(qb.at[d], R_Q + d)

    pass_own(0)
    send(res_ref.at[theirs, :], resb.at[1], dev(dc=1), R_RES)
    send(gate_ref, gateb.at[1], dev(dc=1), R_GATE)
    send(w_ref.at[:, wcols], wb.at[0, c], dev(dc=1), R_WO)
    for d in (1, 2, 3):
        arrived(wb.at[d, c, wrow, pl.ds(pl.multiple_of(wcol, FC), FC)], R_WZ + d)
    wslice = wb.at[pl.ds(1, 3), c, wrow, pl.ds(pl.multiple_of(wcol, FC), FC)]
    for d in (1, 2, 3):
        send(wslice, wslice, dev(dx=d), R_WX + d)
    queries(0)
    whole(0)
    items([(0, 0)])
    pass_own(1)
    pass_own(3)
    pass_other(0)
    for d in (1, 2, 3):
        arrived(wslice, R_WX + d)
    wblock = wb.at[pl.ds(1, 3), c, pl.ds(pl.multiple_of(y * 32, 32), 32), :]
    for d in (1, 7, 2, 6, 3, 5, 4):
        send(wblock, wblock, dev(dy=d), R_WY + d)
    whole(1)
    whole(3)
    whole(4)
    items([(0, 1), (0, 3), (0, 4)])
    queries(1)
    queries(3)
    items([(1, 0), (1, 1), (1, 3), (1, 4), (3, 0), (3, 1), (3, 3), (3, 4)])
    pass_own(2)
    pass_other(1)
    whole(2)
    whole(5)
    items([(0, 2), (1, 2), (3, 2), (0, 5), (1, 5), (3, 5)])
    queries(2)
    items([(2, 0), (2, 1), (2, 2), (2, 3), (2, 4), (2, 5)])
    pass_other(3)
    whole(7)
    items([(0, 7), (1, 7), (3, 7), (2, 7)])
    pass_other(2)
    whole(6)

    def finish(i):
        attend(i, 6)
        ob[i] = (acc[i, :, :HD] / acc[i, :, HD:]).astype(BF)

    def give(i):
        if i == 0:
            send(ob.at[0], att.at[3, 0], dev(dzh=1), R_G3 + 0)
            send(ob.at[0], att.at[1, 0], dev(dzh=3), R_G1 + 0)
        else:
            send(ob.at[i], att.at[0, 4 - i], dev(dx=i), R_RET + 4 - i)

    finish(0)
    finish(1)
    give(0)
    finish(3)
    give(1)
    finish(2)
    give(3)
    att[0, 0] = ob[0]
    give(2)

    ORDER = (0, 3, 1, 2)
    for u in ORDER[1:]:
        arrived(att.at[0, u], R_RET + u)
        send(att.at[0, u], att.at[3, u], dev(dzh=1), R_G3 + u)
        send(att.at[0, u], att.at[1, u], dev(dzh=3), R_G1 + u)

    def wrows(d, u):
        head = (x + u) % NX
        return wb[d, head // 2, pl.ds(pl.multiple_of((head % 2) * HD, HD), HD), :]

    def project(pairs, start=False):
        a = jnp.concatenate([att[d, u] for d, u in pairs], axis=1)
        w = jnp.concatenate([wrows(d, u) for d, u in pairs], axis=0)
        r = jnp.dot(a, w, preferred_element_type=F32)
        oacc[...] = r if start else oacc[...] + r

    arrived(wb.at[0, c], R_WL)
    arrived(wb.at[0, 1 - c], R_WO)
    project([(0, 0), (0, 1), (0, 2), (0, 3)], True)

    lo, hi = pl.ds(0, HALF // 2), pl.ds(HALF // 2, HALF // 2)

    def relay(u):
        arrived(att.at[3, u], R_G3 + u)
        send(att.at[3, u, lo, :], att.at[2, u, lo, :], dev(dzh=1), R_H + u)
        arrived(att.at[1, u], R_G1 + u)
        send(att.at[1, u, hi, :], att.at[2, u, hi, :], dev(dzh=3), R_H + 4 + u)

    relay(0)
    relay(3)
    for d in range(1, NY):
        arrived(wblock, R_WY + d)
    send(wb.at[pl.ds(1, 3), c], wb.at[pl.ds(1, 3), c], dev(dc=1), R_WP)
    relay(1)
    relay(2)
    arrived(wb.at[pl.ds(1, 3), 1 - c], R_WP)
    project([(3, 0), (3, 1), (3, 2), (3, 3)])
    project([(1, 0), (1, 1), (1, 2), (1, 3)])

    def last(us):
        for u in us:
            arrived(att.at[2, u, lo, :], R_H + u)
            arrived(att.at[2, u, hi, :], R_H + 4 + u)
        project([(2, u) for u in us])

    last((0, 3))
    last((1,))
    last((2,))

    arrived(resb.at[0], R_RL)
    arrived(resb.at[1], R_RES)
    arrived(gateb.at[0], R_GL)
    arrived(gateb.at[1], R_GATE)
    for n, core in ((1, 1 - c), (0, c)):
        part = oacc[:, pl.ds(pl.multiple_of(core * FC, FC), FC)]
        mixb[n] = (resb[n].astype(F32) + gateb[n] * part).astype(BF)
    send(mixb.at[1], out_ref.at[mine, :], dev(dc=1), R_OUT)
    local(mixb.at[0], out_ref.at[mine, :], R_OL)
    arrived(out_ref.at[mine, :], R_OL)
    arrived(out_ref.at[theirs, :], R_OUT)

    for here, parts, rows, cols, base, recv, xd, r in waits:
        @pl.when(jnp.logical_not(here))
        def _(parts=parts, rows=rows, cols=cols, recv=recv, base=base, xd=xd, r=r):
            for n, (src, dst) in enumerate(parts):
                pltpu.make_async_remote_copy(
                    src_ref=src.at[rows, cols], dst_ref=dst, send_sem=ss.at[base + n],
                    recv_sem=rs.at[recv], device_id=dev_abs(xd, r),
                    device_id_type=MESH).wait_send()
    for copy in sends:
        copy.wait_send()


N_SEND = 96


def body(queries, keys, values, residual, gate, out_weight):
    return pl.pallas_call(
        kernel,
        out_shape=jax.ShapeDtypeStruct((TOK, FC), BF),
        in_specs=[pl.BlockSpec(memory_space=pl.ANY)] * 6,
        out_specs=pl.BlockSpec(memory_space=pl.ANY),
        scratch_shapes=[
            pltpu.VMEM((NX, HALF, HD), BF),
            pltpu.VMEM((2 * NX, 2, TOK, HD), BF),
            pltpu.VMEM((NZH, NX, HALF, HD), BF),
            pltpu.VMEM((NX, HALF, HD), BF),
            pltpu.VMEM((NZH, 2, 256, FEAT), BF),
            pltpu.VMEM((2, HALF, FC), BF),
            pltpu.VMEM((2, 1, FC), F32),
            pltpu.VMEM((NX, HALF, HD), F32),
            pltpu.VMEM((NX, HALF, 2 * HD), F32),
            pltpu.VMEM((HALF, FEAT), F32),
            pltpu.VMEM((2, HALF, FC), BF),
            pltpu.SemaphoreType.DMA((N_SEND,)),
            pltpu.SemaphoreType.DMA((N_RECV,)),
        ],
        compiler_params=pltpu.CompilerParams(
            collective_id=0, has_side_effects=True, vmem_limit_bytes=60 * 2**20),
        name="attention",
    )(queries, keys, values, residual, gate.reshape(1, FC), out_weight)


def solution(mesh):
    return jax.shard_map(
        body,
        mesh=mesh,
        in_specs=(
            P("ctx", "tp"),
            P("ctx", "tp"),
            P("ctx", "tp"),
            P("ctx", "tp"),
            P("tp"),
            P("tp", None),
        ),
        out_specs=P("ctx", "tp"),
        check_vma=False,
    )
```

```python
import functools
import math

import jax
import jax.numpy as jnp
from jax import lax
from jax.experimental import pallas as pl
from jax.experimental.pallas import tpu as pltpu
from jax.sharding import PartitionSpec as P

MESH = pl.DeviceIdType.MESH
HD = 128
NX, NZL, NY, NZH = 4, 2, 8, 4
TOK = 768
HALF = TOK // 2
FEAT = 768
FC = FEAT // 2
SCALE = math.log2(math.e) / math.sqrt(HD)
BF = jnp.bfloat16
F32 = jnp.float32

R_A, R_B, R_Z, R_Q = 0, 4, 12, 16
R_RET, R_G3, R_G1, R_H = 20, 24, 28, 32
R_WZ, R_WX, R_WY, R_WP, R_WO, R_WL = 40, 44, 48, 56, 57, 58
R_RES, R_GATE, R_RL, R_GL, R_OUT, R_OL = 59, 60, 61, 62, 63, 64
N_RECV = 65


def kernel(q_ref, k_ref, v_ref, res_ref, gate_ref, w_ref, out_ref,
           qb, kv, att, ob, wb, resb, gate0, gate1, mst, acc, s0, s1, newb, alpb, oacc, mixb, ss, rs):
    ctx = lax.axis_index("ctx")
    tp = lax.axis_index("tp")
    x, zl, y = ctx // (NZL * NY), (ctx // NY) % NZL, ctx % NY
    zh, c = tp // 2, tp % 2

    def dev(dx=0, dzl=0, dy=0, dzh=0, dc=0):
        return ((((x + dx) % NX) * NZL + (zl + dzl) % NZL) * NY + (y + dy) % NY,
                ((zh + dzh) % NZH) * 2 + (c + dc) % 2)

    def dev_abs(xd, r):
        return ((xd * NZL + zl) * NY + y, zh * 2 + r)

    sends = []
    count = [0]

    def send(src, dst, device, recv):
        i = count[0]
        count[0] += 1
        copy = pltpu.make_async_remote_copy(
            src_ref=src, dst_ref=dst, send_sem=ss.at[i], recv_sem=rs.at[recv],
            device_id=device, device_id_type=MESH)
        copy.start()
        sends.append(copy)

    def local(src, dst, recv):
        pltpu.make_async_copy(src, dst, rs.at[recv]).start()

    def arrived(dst, recv):
        pltpu.make_async_copy(dst, dst, rs.at[recv]).wait()

    mine = pl.ds(pl.multiple_of(c * HALF, HALF), HALF)
    theirs = pl.ds(pl.multiple_of((1 - c) * HALF, HALF), HALF)
    wcols = pl.ds(pl.multiple_of(zh * FEAT, FEAT), FEAT)

    local(w_ref.at[:, wcols], wb.at[0, c], R_WL)
    local(res_ref.at[mine, :], resb.at[0], R_RL)
    local(gate_ref, gate0, R_GL)

    peers = [dev(dx=d, dc=e) for d in (1, 2, 3) for e in (0, 1)]
    peers += [dev(dc=1), dev(dzl=1)]
    peers += [dev(dzh=d) for d in (1, 2, 3)]
    peers += [dev(dy=d) for d in range(1, NY)]
    barrier = pltpu.get_barrier_semaphore()
    for peer in peers:
        pl.semaphore_signal(barrier, inc=1, device_id=peer, device_id_type=MESH)
    pl.semaphore_wait(barrier, len(peers))

    wrow = pl.ds(pl.multiple_of(y * 32 + (x % 2) * 16, 16), 16)
    wcol = (x // 2) * FC
    for d in (1, 2, 3):
        zd = (zh + d) % NZH
        send(w_ref.at[wrow, pl.ds(pl.multiple_of(zd * FEAT + wcol, FC), FC)],
             wb.at[4 - d, c, wrow, pl.ds(pl.multiple_of(wcol, FC), FC)],
             dev(dzh=d), R_WZ + 4 - d)

    first = jnp.where((2 * c - x) % NX == 2, 1, 0)
    waits = []
    for j in (0, 1):
        head = (j + first) % 2
        xd = 2 * c + head
        slot = (x - xd) % NX
        cols = pl.ds(pl.multiple_of(head * HD, HD), HD)
        for kind in ("kv", "q"):
            for r in (0, 1):
                rows = pl.ds(r * HALF, HALF)
                here = (xd == x) & (c == r)
                if kind == "kv":
                    parts = [(k_ref, kv.at[slot, 0, rows, :]), (v_ref, kv.at[slot, 1, rows, :])]
                    recv = R_A + slot
                else:
                    parts = [(q_ref, qb.at[slot])]
                    recv = R_Q + slot
                base = count[0]
                count[0] += len(parts)

                @pl.when(here)
                def _(parts=parts, rows=rows, cols=cols, recv=recv):
                    for src, dst in parts:
                        pltpu.make_async_copy(src.at[rows, cols], dst, rs.at[recv]).start()

                @pl.when(jnp.logical_not(here))
                def _(parts=parts, rows=rows, cols=cols, recv=recv, base=base, xd=xd, r=r):
                    for n, (src, dst) in enumerate(parts):
                        pltpu.make_async_remote_copy(
                            src_ref=src.at[rows, cols], dst_ref=dst, send_sem=ss.at[base + n],
                            recv_sem=rs.at[recv], device_id=dev_abs(xd, r),
                            device_id_type=MESH).start()

                waits.append((here, parts, rows, cols, base, recv, xd, r))

    def init(n, _):
        mst[n] = jnp.full((HALF, HD), -1e30, F32)
        acc[n] = jnp.zeros((HALF, 2 * HD), F32)
        return 0

    lax.fori_loop(0, NX, init, 0)

    tq = HALF // 2

    def scores(i, s, buf):
        k = kv[s, 0]
        for t in range(HALF // tq):
            rows = pl.ds(t * tq, tq)
            sc = lax.dot_general(qb[i, rows, :], k, (((1,), (1,)), ((), ())),
                                 preferred_element_type=F32)
            (s0, s1)[buf][rows, :] = sc
            old = mst[i, rows, :]
            new = jnp.maximum(old, jnp.max(sc, axis=1, keepdims=True) * SCALE)
            mst[i, rows, :] = new
            newb[buf, rows, :] = new
            alpb[buf, rows, :] = jnp.exp2(old - new)

    def absorb(i, s, buf):
        v = jnp.concatenate([kv[s, 1], jnp.ones((TOK, HD), BF)], axis=1)
        for t in range(HALF // tq):
            rows = pl.ds(t * tq, tq)
            new = newb[buf, rows, :]
            alpha = alpb[buf, rows, :]
            p = jnp.exp2((s0, s1)[buf][rows, :] * SCALE
                         - jnp.concatenate([new] * (TOK // HD), axis=1)).astype(BF)
            pv = jnp.dot(p, v, preferred_element_type=F32)
            acc[i, rows, :] = acc[i, rows, :] * jnp.concatenate([alpha, alpha], axis=1) + pv

    pending = []

    def step(i, s):
        buf = len(pending) % 2
        scores(i, s, buf)
        if pending:
            absorb(*pending[-1], 1 - buf)
        pending.append((i, s))

    def items(pairs):
        assert len(pending) % 2 == 1 and len(pairs) % 2 == 0
        seq = [pending[-1]] + pairs
        icode = sum(i << (2 * n) for n, (i, _) in enumerate(seq))
        scode = sum(s << (3 * n) for n, (_, s) in enumerate(seq))

        def at(n):
            return (jnp.int32(icode) >> (2 * n)) & 3, (jnp.int32(scode) >> (3 * n)) & 7

        def body(n, _):
            a, b, d = at(2 * n), at(2 * n + 1), at(2 * n + 2)
            scores(*b, 1)
            absorb(*a, 0)
            scores(*d, 0)
            absorb(*b, 1)
            return 0

        lax.fori_loop(0, len(pairs) // 2, body, 0)
        pending.extend(pairs)

    def half_of(s, rows):
        return kv.at[s, :, rows, :]

    def pass_own(d):
        arrived(half_of(d, mine), R_A + d)
        send(half_of(d, mine), half_of(d, mine), dev(dc=1), R_B + d)
        send(half_of(d, mine), half_of(4 + d, mine), dev(dzl=1), R_Z + d)

    def pass_other(d):
        arrived(half_of(4 + d, mine), R_Z + d)
        send(half_of(4 + d, mine), half_of(4 + d, mine), dev(dc=1), R_B + 4 + d)

    def whole(s):
        arrived(half_of(s, theirs), R_B + s)

    def queries(d):
        arrived(qb.at[d], R_Q + d)

    pass_own(0)
    send(res_ref.at[theirs, :], resb.at[1], dev(dc=1), R_RES)
    send(gate_ref, gate1, dev(dc=1), R_GATE)
    send(w_ref.at[:, wcols], wb.at[0, c], dev(dc=1), R_WO)
    for d in (1, 2, 3):
        arrived(wb.at[d, c, wrow, pl.ds(pl.multiple_of(wcol, FC), FC)], R_WZ + d)
    wslice = wb.at[pl.ds(1, 3), c, wrow, pl.ds(pl.multiple_of(wcol, FC), FC)]
    for d in (1, 2, 3):
        send(wslice, wslice, dev(dx=d), R_WX + d)
    queries(0)
    whole(0)
    step(0, 0)
    pass_own(1)
    pass_own(3)
    pass_other(0)
    for d in (1, 2, 3):
        arrived(wslice, R_WX + d)
    wblock = wb.at[pl.ds(1, 3), c, pl.ds(pl.multiple_of(y * 32, 32), 32), :]
    for d in (1, 7, 2, 6, 3, 5, 4):
        send(wblock, wblock, dev(dy=d), R_WY + d)
    whole(1)
    whole(3)
    whole(4)
    items([(0, 1), (0, 3)])
    queries(1)
    queries(3)
    items([(0, 4), (1, 0), (1, 1), (1, 3), (1, 4), (3, 0), (3, 1), (3, 3)])
    pass_own(2)
    pass_other(1)
    whole(2)
    whole(5)
    items([(3, 4), (0, 2), (1, 2), (3, 2), (0, 5), (1, 5)])
    queries(2)
    items([(3, 5), (2, 0), (2, 1), (2, 2), (2, 3), (2, 4)])
    pass_other(3)
    whole(7)
    items([(2, 5), (0, 7), (1, 7), (3, 7)])
    step(2, 7)
    pass_other(2)
    whole(6)

    def finish(i):
        ob[i] = (acc[i, :, :HD] / acc[i, :, HD:]).astype(BF)

    def give(i):
        if i == 0:
            send(ob.at[0], att.at[3, 0], dev(dzh=1), R_G3 + 0)
            send(ob.at[0], att.at[1, 0], dev(dzh=3), R_G1 + 0)
        else:
            send(ob.at[i], att.at[0, 4 - i], dev(dx=i), R_RET + 4 - i)

    step(0, 6)
    step(1, 6)
    finish(0)
    step(3, 6)
    finish(1)
    give(0)
    step(2, 6)
    finish(3)
    give(1)
    absorb(*pending[-1], (len(pending) - 1) % 2)
    finish(2)
    give(3)
    att[0, 0] = ob[0]
    give(2)

    ORDER = (0, 3, 1, 2)
    for u in ORDER[1:]:
        arrived(att.at[0, u], R_RET + u)
        send(att.at[0, u], att.at[3, u], dev(dzh=1), R_G3 + u)
        send(att.at[0, u], att.at[1, u], dev(dzh=3), R_G1 + u)

    def wrows(d, u):
        head = (x + u) % NX
        return wb[d, head // 2, pl.ds(pl.multiple_of((head % 2) * HD, HD), HD), :]

    def project(pairs, start=False):
        a = jnp.concatenate([att[d, u] for d, u in pairs], axis=1)
        w = jnp.concatenate([wrows(d, u) for d, u in pairs], axis=0)
        r = jnp.dot(a, w, preferred_element_type=F32)
        oacc[...] = r if start else oacc[...] + r

    arrived(wb.at[0, c], R_WL)
    arrived(wb.at[0, 1 - c], R_WO)
    project([(0, 0), (0, 1), (0, 2), (0, 3)], True)

    lo, hi = pl.ds(0, HALF // 2), pl.ds(HALF // 2, HALF // 2)

    def relay(u):
        arrived(att.at[3, u], R_G3 + u)
        send(att.at[3, u, lo, :], att.at[2, u, lo, :], dev(dzh=1), R_H + u)
        arrived(att.at[1, u], R_G1 + u)
        send(att.at[1, u, hi, :], att.at[2, u, hi, :], dev(dzh=3), R_H + 4 + u)

    relay(0)
    relay(3)
    for d in range(1, NY):
        arrived(wblock, R_WY + d)
    send(wb.at[pl.ds(1, 3), c], wb.at[pl.ds(1, 3), c], dev(dc=1), R_WP)
    relay(1)
    relay(2)
    arrived(wb.at[pl.ds(1, 3), 1 - c], R_WP)
    project([(3, 0), (3, 1), (3, 2), (3, 3)])
    project([(1, 0), (1, 1), (1, 2), (1, 3)])

    def last(us):
        for u in us:
            arrived(att.at[2, u, lo, :], R_H + u)
            arrived(att.at[2, u, hi, :], R_H + 4 + u)
        project([(2, u) for u in us])

    last((0, 3))
    last((1,))
    last((2,))

    arrived(resb.at[0], R_RL)
    arrived(resb.at[1], R_RES)
    arrived(gate0, R_GL)
    arrived(gate1, R_GATE)
    for n, core, g in ((1, 1 - c, gate1), (0, c, gate0)):
        part = oacc[:, pl.ds(pl.multiple_of(core * FC, FC), FC)]
        mixb[n] = (resb[n].astype(F32) + g[...].reshape(1, FC) * part).astype(BF)
    send(mixb.at[1], out_ref.at[mine, :], dev(dc=1), R_OUT)
    local(mixb.at[0], out_ref.at[mine, :], R_OL)
    arrived(out_ref.at[mine, :], R_OL)
    arrived(out_ref.at[theirs, :], R_OUT)

    for here, parts, rows, cols, base, recv, xd, r in waits:
        @pl.when(jnp.logical_not(here))
        def _(parts=parts, rows=rows, cols=cols, recv=recv, base=base, xd=xd, r=r):
            for n, (src, dst) in enumerate(parts):
                pltpu.make_async_remote_copy(
                    src_ref=src.at[rows, cols], dst_ref=dst, send_sem=ss.at[base + n],
                    recv_sem=rs.at[recv], device_id=dev_abs(xd, r),
                    device_id_type=MESH).wait_send()
    for copy in sends:
        copy.wait_send()


N_SEND = 96


def body(queries, keys, values, residual, gate, out_weight):
    return pl.pallas_call(
        kernel,
        out_shape=jax.ShapeDtypeStruct((TOK, FC), BF),
        in_specs=[pl.BlockSpec(memory_space=pl.ANY)] * 6,
        out_specs=pl.BlockSpec(memory_space=pl.ANY),
        scratch_shapes=[
            pltpu.VMEM((NX, HALF, HD), BF),
            pltpu.VMEM((2 * NX, 2, TOK, HD), BF),
            pltpu.VMEM((NZH, NX, HALF, HD), BF),
            pltpu.VMEM((NX, HALF, HD), BF),
            pltpu.VMEM((NZH, 2, 256, FEAT), BF),
            pltpu.VMEM((2, HALF, FC), BF),
            pltpu.VMEM((FC,), F32),
            pltpu.VMEM((FC,), F32),
            pltpu.VMEM((NX, HALF, HD), F32),
            pltpu.VMEM((NX, HALF, 2 * HD), F32),
            pltpu.VMEM((HALF, TOK), F32),
            pltpu.VMEM((HALF, TOK), F32),
            pltpu.VMEM((2, HALF, HD), F32),
            pltpu.VMEM((2, HALF, HD), F32),
            pltpu.VMEM((HALF, FEAT), F32),
            pltpu.VMEM((2, HALF, FC), BF),
            pltpu.SemaphoreType.DMA((N_SEND,)),
            pltpu.SemaphoreType.DMA((N_RECV,)),
        ],
        compiler_params=pltpu.CompilerParams(
            collective_id=0, has_side_effects=True, vmem_limit_bytes=60 * 2**20),
        name="attention",
    )(queries, keys, values, residual, gate, out_weight)


def solution(mesh):
    return jax.shard_map(
        body,
        mesh=mesh,
        in_specs=(
            P("ctx", "tp"),
            P("ctx", "tp"),
            P("ctx", "tp"),
            P("ctx", "tp"),
            P("tp"),
            P("tp", None),
        ),
        out_specs=P("ctx", "tp"),
        check_vma=False,
    )
```

```python
import functools
import math

import jax
import jax.numpy as jnp
from jax import lax
from jax.experimental import pallas as pl
from jax.experimental.pallas import tpu as pltpu
from jax.sharding import PartitionSpec as P

MESH = pl.DeviceIdType.MESH
HD = 128
NX, NZL, NY, NZH = 4, 2, 8, 4
TOK = 768
HALF = TOK // 2
FEAT = 768
FC = FEAT // 2
SCALE = math.log2(math.e) / math.sqrt(HD)
BF = jnp.bfloat16
F32 = jnp.float32

R_A, R_B, R_Z, R_Q = 0, 4, 12, 16
R_RET, R_G3, R_G1, R_H = 20, 24, 28, 32
R_WZ, R_WX, R_WY, R_WP, R_WO, R_WL = 40, 44, 48, 56, 57, 58
R_RES, R_GATE, R_RL, R_GL, R_OUT, R_OL = 59, 60, 61, 62, 63, 64
N_RECV = 65


def kernel(q_ref, k_ref, v_ref, w_ref, out_ref,
           qb, kv, att, ob, wb, mst, acc, s0, s1, newb, alpb, oacc, mixb, ss, rs):
    ctx = lax.axis_index("ctx")
    tp = lax.axis_index("tp")
    x, zl, y = ctx // (NZL * NY), (ctx // NY) % NZL, ctx % NY
    zh, c = tp // 2, tp % 2

    def dev(dx=0, dzl=0, dy=0, dzh=0, dc=0):
        return ((((x + dx) % NX) * NZL + (zl + dzl) % NZL) * NY + (y + dy) % NY,
                ((zh + dzh) % NZH) * 2 + (c + dc) % 2)

    def dev_abs(xd, r):
        return ((xd * NZL + zl) * NY + y, zh * 2 + r)

    sends = []
    count = [0]

    def send(src, dst, device, recv):
        i = count[0]
        count[0] += 1
        copy = pltpu.make_async_remote_copy(
            src_ref=src, dst_ref=dst, send_sem=ss.at[i], recv_sem=rs.at[recv],
            device_id=device, device_id_type=MESH)
        copy.start()
        sends.append(copy)

    def local(src, dst, recv):
        pltpu.make_async_copy(src, dst, rs.at[recv]).start()

    def arrived(dst, recv):
        pltpu.make_async_copy(dst, dst, rs.at[recv]).wait()

    mine = pl.ds(pl.multiple_of(c * HALF, HALF), HALF)
    theirs = pl.ds(pl.multiple_of((1 - c) * HALF, HALF), HALF)
    wcols = pl.ds(pl.multiple_of(zh * FEAT, FEAT), FEAT)

    local(w_ref.at[:, wcols], wb.at[0, c], R_WL)

    peers = [dev(dx=d, dc=e) for d in (1, 2, 3) for e in (0, 1)]
    peers += [dev(dc=1), dev(dzl=1)]
    peers += [dev(dzh=d) for d in (1, 2, 3)]
    peers += [dev(dy=d) for d in range(1, NY)]
    barrier = pltpu.get_barrier_semaphore()
    for peer in peers:
        pl.semaphore_signal(barrier, inc=1, device_id=peer, device_id_type=MESH)
    pl.semaphore_wait(barrier, len(peers))

    wrow = pl.ds(pl.multiple_of(y * 32 + (x % 2) * 16, 16), 16)
    wcol = (x // 2) * FC
    for d in (1, 2, 3):
        zd = (zh + d) % NZH
        send(w_ref.at[wrow, pl.ds(pl.multiple_of(zd * FEAT + wcol, FC), FC)],
             wb.at[4 - d, c, wrow, pl.ds(pl.multiple_of(wcol, FC), FC)],
             dev(dzh=d), R_WZ + 4 - d)

    first = jnp.where((2 * c - x) % NX == 2, 1, 0)
    waits = []

    def exchange(j, when):
        head = (j + first) % 2
        xd = 2 * c + head
        slot = (x - xd) % NX
        cols = pl.ds(pl.multiple_of(head * HD, HD), HD)
        for kind in ("kv", "q"):
            for r in (0, 1):
                rows = pl.ds(r * HALF, HALF)
                here = (xd == x) & (c == r)
                if kind == "kv":
                    parts = [(k_ref, kv.at[slot, 0, rows, :]), (v_ref, kv.at[slot, 1, rows, :])]
                    recv = R_A + slot
                else:
                    parts = [(q_ref, qb.at[slot])]
                    recv = R_Q + slot
                base = count[0]
                count[0] += len(parts)

                def remote(do, parts=parts, rows=rows, base=base, recv=recv, r=r):
                    for n, (src, dst) in enumerate(parts):
                        do(pltpu.make_async_remote_copy(
                            src_ref=src.at[rows, cols], dst_ref=dst, send_sem=ss.at[base + n],
                            recv_sem=rs.at[recv], device_id=dev_abs(xd, r),
                            device_id_type=MESH))

                @pl.when(here & when)
                def _():
                    for src, dst in parts:
                        pltpu.make_async_copy(src.at[rows, cols], dst, rs.at[recv]).start()

                @pl.when(jnp.logical_not(here) & when)
                def _():
                    remote(lambda copy: copy.start())

                def drain(remote=remote, here=here, when=when):
                    @pl.when(jnp.logical_not(here) & when)
                    def _():
                        remote(lambda copy: copy.wait_send())

                waits.append(drain)

    far = (x - 2 * c - (1 + first) % 2) % NX == 2
    always = c >= 0
    exchange(0, always)
    exchange(1, jnp.logical_not(far))

    def init(n, _):
        mst[n] = jnp.full((HALF, HD), -1e30, F32)
        acc[n] = jnp.zeros((HALF, 2 * HD), F32)
        return 0

    lax.fori_loop(0, NX, init, 0)

    tq = HALF // 2

    def scores(i, s, buf):
        k = kv[s, 0]
        for t in range(HALF // tq):
            rows = pl.ds(t * tq, tq)
            sc = lax.dot_general(qb[i, rows, :], k, (((1,), (1,)), ((), ())),
                                 preferred_element_type=F32)
            (s0, s1)[buf][rows, :] = sc
            old = mst[i, rows, :]
            new = jnp.maximum(old, jnp.max(sc, axis=1, keepdims=True) * SCALE)
            mst[i, rows, :] = new
            newb[buf, rows, :] = new
            alpb[buf, rows, :] = jnp.exp2(old - new)

    def absorb(i, s, buf):
        v = jnp.concatenate([kv[s, 1], jnp.ones((TOK, HD), BF)], axis=1)
        for t in range(HALF // tq):
            rows = pl.ds(t * tq, tq)
            new = newb[buf, rows, :]
            alpha = alpb[buf, rows, :]
            p = jnp.exp2((s0, s1)[buf][rows, :] * SCALE
                         - jnp.concatenate([new] * (TOK // HD), axis=1)).astype(BF)
            pv = jnp.dot(p, v, preferred_element_type=F32)
            acc[i, rows, :] = acc[i, rows, :] * jnp.concatenate([alpha, alpha], axis=1) + pv

    pending = []

    def step(i, s):
        buf = len(pending) % 2
        scores(i, s, buf)
        if pending:
            absorb(*pending[-1], 1 - buf)
        pending.append((i, s))

    def items(pairs):
        assert len(pending) % 2 == 1 and len(pairs) % 2 == 0
        seq = [pending[-1]] + pairs
        icode = sum(i << (2 * n) for n, (i, _) in enumerate(seq))
        scode = sum(s << (3 * n) for n, (_, s) in enumerate(seq))

        def at(n):
            return (jnp.int32(icode) >> (2 * n)) & 3, (jnp.int32(scode) >> (3 * n)) & 7

        def body(n, _):
            a, b, d = at(2 * n), at(2 * n + 1), at(2 * n + 2)
            scores(*b, 1)
            absorb(*a, 0)
            scores(*d, 0)
            absorb(*b, 1)
            return 0

        lax.fori_loop(0, len(pairs) // 2, body, 0)
        pending.extend(pairs)

    def half_of(s, rows):
        return kv.at[s, :, rows, :]

    def pass_own(d):
        arrived(half_of(d, mine), R_A + d)
        send(half_of(d, mine), half_of(d, mine), dev(dc=1), R_B + d)
        send(half_of(d, mine), half_of(4 + d, mine), dev(dzl=1), R_Z + d)

    def pass_other(d):
        arrived(half_of(4 + d, mine), R_Z + d)
        send(half_of(4 + d, mine), half_of(4 + d, mine), dev(dc=1), R_B + 4 + d)

    def whole(s):
        arrived(half_of(s, theirs), R_B + s)

    def queries(d):
        arrived(qb.at[d], R_Q + d)

    pass_own(0)
    send(w_ref.at[:, wcols], wb.at[0, c], dev(dc=1), R_WO)
    queries(0)
    whole(0)
    step(0, 0)
    for d in (1, 2, 3):
        arrived(wb.at[d, c, wrow, pl.ds(pl.multiple_of(wcol, FC), FC)], R_WZ + d)
    wslice = wb.at[pl.ds(1, 3), c, wrow, pl.ds(pl.multiple_of(wcol, FC), FC)]
    for d in (1, 3, 2):
        send(wslice, wslice, dev(dx=d), R_WX + d)
    exchange(1, far)
    pass_own(1)
    pass_own(3)
    pass_other(0)
    whole(1)
    whole(3)
    items([(0, 1), (0, 3)])
    for d in (1, 2, 3):
        arrived(wslice, R_WX + d)
    wblock = wb.at[pl.ds(1, 3), c, pl.ds(pl.multiple_of(y * 32, 32), 32), :]
    for d in (4, 3, 5, 2, 6, 1, 7):
        send(wblock, wblock, dev(dy=d), R_WY + d)
    whole(4)
    queries(1)
    queries(3)
    items([(0, 4), (1, 0), (1, 1), (1, 3), (1, 4), (3, 0)])
    pass_other(1)
    items([(3, 1), (3, 3)])
    pass_own(2)
    whole(5)
    whole(2)
    items([(3, 4), (0, 5), (1, 5), (3, 5), (0, 2), (1, 2)])
    queries(2)
    pass_other(3)
    items([(3, 2), (2, 0), (2, 1), (2, 3), (2, 4), (2, 5)])
    whole(7)
    items([(2, 2), (0, 7)])
    pass_other(2)
    items([(1, 7), (3, 7)])
    step(2, 7)
    whole(6)

    def finish(i):
        ob[i] = (acc[i, :, :HD] / acc[i, :, HD:]).astype(BF)

    def give(i):
        if i == 0:
            send(ob.at[0], att.at[3, 0], dev(dzh=1), R_G3 + 0)
            send(ob.at[0], att.at[1, 0], dev(dzh=3), R_G1 + 0)
        else:
            send(ob.at[i], att.at[0, 4 - i], dev(dx=i), R_RET + 4 - i)

    step(0, 6)
    step(1, 6)
    finish(0)
    step(3, 6)
    finish(1)
    give(0)
    step(2, 6)
    finish(3)
    give(1)
    absorb(*pending[-1], (len(pending) - 1) % 2)
    finish(2)
    give(3)
    att[0, 0] = ob[0]
    give(2)

    ORDER = (0, 3, 1, 2)
    for u in ORDER[1:]:
        arrived(att.at[0, u], R_RET + u)
        send(att.at[0, u], att.at[3, u], dev(dzh=1), R_G3 + u)
        send(att.at[0, u], att.at[1, u], dev(dzh=3), R_G1 + u)

    def wrows(d, u):
        head = (x + u) % NX
        return wb[d, head // 2, pl.ds(pl.multiple_of((head % 2) * HD, HD), HD), :]

    def project(pairs, start=False):
        a = jnp.concatenate([att[d, u] for d, u in pairs], axis=1)
        w = jnp.concatenate([wrows(d, u) for d, u in pairs], axis=0)
        r = jnp.dot(a, w, preferred_element_type=F32)
        oacc[...] = r if start else oacc[...] + r

    arrived(wb.at[0, c], R_WL)
    arrived(wb.at[0, 1 - c], R_WO)
    project([(0, 0), (0, 1), (0, 2), (0, 3)], True)

    lo, hi = pl.ds(0, HALF // 2), pl.ds(HALF // 2, HALF // 2)

    def relay(u):
        arrived(att.at[3, u], R_G3 + u)
        send(att.at[3, u, lo, :], att.at[2, u, lo, :], dev(dzh=1), R_H + u)
        arrived(att.at[1, u], R_G1 + u)
        send(att.at[1, u, hi, :], att.at[2, u, hi, :], dev(dzh=3), R_H + 4 + u)

    relay(0)
    relay(3)
    for d in range(1, NY):
        arrived(wblock, R_WY + d)
    send(wb.at[pl.ds(1, 3), c], wb.at[pl.ds(1, 3), c], dev(dc=1), R_WP)
    relay(1)
    relay(2)
    arrived(wb.at[pl.ds(1, 3), 1 - c], R_WP)
    project([(3, 0), (3, 1), (3, 2), (3, 3)])
    project([(1, 0), (1, 1), (1, 2), (1, 3)])

    def last(us):
        for u in us:
            arrived(att.at[2, u, lo, :], R_H + u)
            arrived(att.at[2, u, hi, :], R_H + 4 + u)
        project([(2, u) for u in us])

    last((0, 3))
    last((1,))
    last((2,))

    for n, core in ((1, 1 - c), (0, c)):
        mixb[n] = oacc[:, pl.ds(pl.multiple_of(core * FC, FC), FC)].astype(BF)
    send(mixb.at[1], out_ref.at[mine, :], dev(dc=1), R_OUT)
    local(mixb.at[0], out_ref.at[mine, :], R_OL)
    arrived(out_ref.at[mine, :], R_OL)
    arrived(out_ref.at[theirs, :], R_OUT)

    for drain in waits:
        drain()
    for copy in sends:
        copy.wait_send()


N_SEND = 96


def body(queries, keys, values, residual, gate, out_weight):
    projected = pl.pallas_call(
        kernel,
        out_shape=jax.ShapeDtypeStruct((TOK, FC), BF),
        in_specs=[pl.BlockSpec(memory_space=pl.ANY)] * 4,
        out_specs=pl.BlockSpec(memory_space=pl.ANY),
        scratch_shapes=[
            pltpu.VMEM((NX, HALF, HD), BF),
            pltpu.VMEM((2 * NX, 2, TOK, HD), BF),
            pltpu.VMEM((NZH, NX, HALF, HD), BF),
            pltpu.VMEM((NX, HALF, HD), BF),
            pltpu.VMEM((NZH, 2, 256, FEAT), BF),
            pltpu.VMEM((NX, HALF, HD), F32),
            pltpu.VMEM((NX, HALF, 2 * HD), F32),
            pltpu.VMEM((HALF, TOK), F32),
            pltpu.VMEM((HALF, TOK), F32),
            pltpu.VMEM((2, HALF, HD), F32),
            pltpu.VMEM((2, HALF, HD), F32),
            pltpu.VMEM((HALF, FEAT), F32),
            pltpu.VMEM((2, HALF, FC), BF),
            pltpu.SemaphoreType.DMA((N_SEND,)),
            pltpu.SemaphoreType.DMA((N_RECV,)),
        ],
        compiler_params=pltpu.CompilerParams(
            collective_id=0, has_side_effects=True, vmem_limit_bytes=60 * 2**20),
        name="attention",
    )(queries, keys, values, out_weight)
    return (residual.astype(F32) + gate[None, :] * projected.astype(F32)).astype(BF)


def solution(mesh):
    return jax.shard_map(
        body,
        mesh=mesh,
        in_specs=(
            P("ctx", "tp"),
            P("ctx", "tp"),
            P("ctx", "tp"),
            P("ctx", "tp"),
            P("tp"),
            P("tp", None),
        ),
        out_specs=P("ctx", "tp"),
        check_vma=False,
    )
```

```python
import functools
import math

import jax
import jax.numpy as jnp
from jax import lax
from jax.experimental import pallas as pl
from jax.experimental.pallas import tpu as pltpu
from jax.sharding import PartitionSpec as P

MESH = pl.DeviceIdType.MESH
HD = 128
NX, NZL, NY, NZH = 4, 2, 8, 4
TOK = 768
HALF = TOK // 2
FEAT = 768
FC = FEAT // 2
SCALE = math.log2(math.e) / math.sqrt(HD)
BF = jnp.bfloat16
F32 = jnp.float32

R_A, R_B, R_Z, R_Q = 0, 4, 12, 16
R_RET, R_G3, R_G1, R_H = 20, 24, 28, 32
R_WZ, R_WX, R_WY, R_WP, R_WO, R_WL = 40, 44, 48, 56, 57, 58
R_RES, R_GATE, R_RL, R_GL, R_OUT, R_OL = 59, 60, 61, 62, 63, 64
N_RECV = 65


def kernel(q_ref, k_ref, v_ref, w_ref, out_ref,
           qb, kv, att, ob, wb, mst, acc, s0, s1, newb, alpb, oacc, mixb, ss, rs):
    ctx = lax.axis_index("ctx")
    tp = lax.axis_index("tp")
    x, zl, y = ctx // (NZL * NY), (ctx // NY) % NZL, ctx % NY
    zh, c = tp // 2, tp % 2

    def dev(dx=0, dzl=0, dy=0, dzh=0, dc=0):
        return ((((x + dx) % NX) * NZL + (zl + dzl) % NZL) * NY + (y + dy) % NY,
                ((zh + dzh) % NZH) * 2 + (c + dc) % 2)

    def dev_abs(xd, r):
        return ((xd * NZL + zl) * NY + y, zh * 2 + r)

    sends = []
    count = [0]

    def send(src, dst, device, recv):
        i = count[0]
        count[0] += 1
        copy = pltpu.make_async_remote_copy(
            src_ref=src, dst_ref=dst, send_sem=ss.at[i], recv_sem=rs.at[recv],
            device_id=device, device_id_type=MESH)
        copy.start()
        sends.append(copy)

    def local(src, dst, recv):
        pltpu.make_async_copy(src, dst, rs.at[recv]).start()

    def arrived(dst, recv):
        pltpu.make_async_copy(dst, dst, rs.at[recv]).wait()

    mine = pl.ds(pl.multiple_of(c * HALF, HALF), HALF)
    theirs = pl.ds(pl.multiple_of((1 - c) * HALF, HALF), HALF)
    wcols = pl.ds(pl.multiple_of(zh * FEAT, FEAT), FEAT)

    local(w_ref.at[:, wcols], wb.at[0, c], R_WL)

    peers = [dev(dx=d, dc=e) for d in (1, 2, 3) for e in (0, 1)]
    peers += [dev(dc=1), dev(dzl=1)]
    peers += [dev(dzh=d) for d in (1, 2, 3)]
    peers += [dev(dy=d) for d in range(1, NY)]
    barrier = pltpu.get_barrier_semaphore()
    for peer in peers:
        pl.semaphore_signal(barrier, inc=1, device_id=peer, device_id_type=MESH)
    pl.semaphore_wait(barrier, len(peers))

    wrow = pl.ds(pl.multiple_of(y * 32 + (x % 2) * 16, 16), 16)
    wcol = (x // 2) * FC
    for d in (1, 2, 3):
        zd = (zh + d) % NZH
        send(w_ref.at[wrow, pl.ds(pl.multiple_of(zd * FEAT + wcol, FC), FC)],
             wb.at[4 - d, c, wrow, pl.ds(pl.multiple_of(wcol, FC), FC)],
             dev(dzh=d), R_WZ + 4 - d)

    first = jnp.where((2 * c - x) % NX == 2, 1, 0)
    waits = []

    def exchange(j, when):
        head = (j + first) % 2
        xd = 2 * c + head
        slot = (x - xd) % NX
        cols = pl.ds(pl.multiple_of(head * HD, HD), HD)
        for kind in ("kv", "q"):
            for r in (0, 1):
                rows = pl.ds(r * HALF, HALF)
                here = (xd == x) & (c == r)
                if kind == "kv":
                    parts = [(k_ref, kv.at[slot, 0, rows, :]), (v_ref, kv.at[slot, 1, rows, :])]
                    recv = R_A + slot
                else:
                    parts = [(q_ref, qb.at[slot])]
                    recv = R_Q + slot
                base = count[0]
                count[0] += len(parts)

                def remote(do, parts=parts, rows=rows, base=base, recv=recv, r=r):
                    for n, (src, dst) in enumerate(parts):
                        do(pltpu.make_async_remote_copy(
                            src_ref=src.at[rows, cols], dst_ref=dst, send_sem=ss.at[base + n],
                            recv_sem=rs.at[recv], device_id=dev_abs(xd, r),
                            device_id_type=MESH))

                @pl.when(here & when)
                def _():
                    for src, dst in parts:
                        pltpu.make_async_copy(src.at[rows, cols], dst, rs.at[recv]).start()

                @pl.when(jnp.logical_not(here) & when)
                def _():
                    remote(lambda copy: copy.start())

                def drain(remote=remote, here=here, when=when):
                    @pl.when(jnp.logical_not(here) & when)
                    def _():
                        remote(lambda copy: copy.wait_send())

                waits.append(drain)

    far = (x - 2 * c - (1 + first) % 2) % NX == 2
    always = c >= 0
    exchange(0, always)
    exchange(1, jnp.logical_not(far))

    def init(n, _):
        mst[n] = jnp.full((HALF, HD), -1e30, F32)
        acc[n] = jnp.zeros((HALF, 2 * HD), F32)
        return 0

    lax.fori_loop(0, NX, init, 0)

    tq = HALF // 2

    def scores(i, s, buf):
        k = kv[s, 0]
        for t in range(HALF // tq):
            rows = pl.ds(t * tq, tq)
            sc = lax.dot_general(qb[i, rows, :], k, (((1,), (1,)), ((), ())),
                                 preferred_element_type=F32)
            (s0, s1)[buf][rows, :] = sc
            old = mst[i, rows, :]
            new = jnp.maximum(old, jnp.max(sc, axis=1, keepdims=True) * SCALE)
            mst[i, rows, :] = new
            newb[buf, rows, :] = new
            alpb[buf, rows, :] = jnp.exp2(old - new)

    def absorb(i, s, buf):
        v = jnp.concatenate([kv[s, 1], jnp.ones((TOK, HD), BF)], axis=1)
        for t in range(HALF // tq):
            rows = pl.ds(t * tq, tq)
            new = newb[buf, rows, :]
            alpha = alpb[buf, rows, :]
            p = jnp.exp2((s0, s1)[buf][rows, :] * SCALE
                         - jnp.concatenate([new] * (TOK // HD), axis=1)).astype(BF)
            pv = jnp.dot(p, v, preferred_element_type=F32)
            acc[i, rows, :] = acc[i, rows, :] * jnp.concatenate([alpha, alpha], axis=1) + pv

    pending = []

    def step(i, s):
        buf = len(pending) % 2
        scores(i, s, buf)
        if pending:
            absorb(*pending[-1], 1 - buf)
        pending.append((i, s))

    def items(pairs):
        for i, n in pairs:
            step(i, n)

    def half_of(s, rows):
        return kv.at[s, :, rows, :]

    def pass_own(d):
        arrived(half_of(d, mine), R_A + d)
        send(half_of(d, mine), half_of(d, mine), dev(dc=1), R_B + d)
        send(half_of(d, mine), half_of(4 + d, mine), dev(dzl=1), R_Z + d)

    def pass_other(d):
        arrived(half_of(4 + d, mine), R_Z + d)
        send(half_of(4 + d, mine), half_of(4 + d, mine), dev(dc=1), R_B + 4 + d)

    def whole(s):
        arrived(half_of(s, theirs), R_B + s)

    def queries(d):
        arrived(qb.at[d], R_Q + d)

    pass_own(0)
    send(w_ref.at[:, wcols], wb.at[0, c], dev(dc=1), R_WO)
    queries(0)
    whole(0)
    step(0, 0)
    for d in (1, 2, 3):
        arrived(wb.at[d, c, wrow, pl.ds(pl.multiple_of(wcol, FC), FC)], R_WZ + d)
    wslice = wb.at[pl.ds(1, 3), c, wrow, pl.ds(pl.multiple_of(wcol, FC), FC)]
    for d in (1, 3, 2):
        send(wslice, wslice, dev(dx=d), R_WX + d)
    exchange(1, far)
    pass_own(1)
    pass_own(3)
    pass_other(0)
    whole(1)
    whole(3)
    items([(0, 1), (0, 3)])
    for d in (1, 2, 3):
        arrived(wslice, R_WX + d)
    wblock = wb.at[pl.ds(1, 3), c, pl.ds(pl.multiple_of(y * 32, 32), 32), :]
    for d in (4, 3, 5, 2, 6, 1, 7):
        send(wblock, wblock, dev(dy=d), R_WY + d)
    whole(4)
    queries(1)
    queries(3)
    items([(0, 4), (1, 0), (1, 1), (1, 3), (1, 4), (3, 0)])
    pass_other(1)
    items([(3, 1), (3, 3)])
    pass_own(2)
    whole(5)
    whole(2)
    items([(3, 4), (0, 5), (1, 5), (3, 5), (0, 2), (1, 2)])
    queries(2)
    pass_other(3)
    items([(3, 2), (2, 0), (2, 1), (2, 3), (2, 4), (2, 5)])
    whole(7)
    items([(2, 2), (0, 7)])
    pass_other(2)
    items([(1, 7), (3, 7)])
    step(2, 7)
    whole(6)

    def finish(i):
        ob[i] = (acc[i, :, :HD] / acc[i, :, HD:]).astype(BF)

    def give(i):
        if i == 0:
            send(ob.at[0], att.at[3, 0], dev(dzh=1), R_G3 + 0)
            send(ob.at[0], att.at[1, 0], dev(dzh=3), R_G1 + 0)
        else:
            send(ob.at[i], att.at[0, 4 - i], dev(dx=i), R_RET + 4 - i)

    step(0, 6)
    step(1, 6)
    finish(0)
    step(3, 6)
    finish(1)
    give(0)
    step(2, 6)
    finish(3)
    give(1)
    absorb(*pending[-1], (len(pending) - 1) % 2)
    finish(2)
    give(3)
    att[0, 0] = ob[0]
    give(2)

    ORDER = (0, 3, 1, 2)
    for u in ORDER[1:]:
        arrived(att.at[0, u], R_RET + u)
        send(att.at[0, u], att.at[3, u], dev(dzh=1), R_G3 + u)
        send(att.at[0, u], att.at[1, u], dev(dzh=3), R_G1 + u)

    def wrows(d, u):
        head = (x + u) % NX
        return wb[d, head // 2, pl.ds(pl.multiple_of((head % 2) * HD, HD), HD), :]

    def project(pairs, start=False):
        a = jnp.concatenate([att[d, u] for d, u in pairs], axis=1)
        w = jnp.concatenate([wrows(d, u) for d, u in pairs], axis=0)
        r = jnp.dot(a, w, preferred_element_type=F32)
        oacc[...] = r if start else oacc[...] + r

    arrived(wb.at[0, c], R_WL)
    arrived(wb.at[0, 1 - c], R_WO)
    project([(0, 0), (0, 1), (0, 2), (0, 3)], True)

    lo, hi = pl.ds(0, HALF // 2), pl.ds(HALF // 2, HALF // 2)

    def relay(u):
        arrived(att.at[3, u], R_G3 + u)
        send(att.at[3, u, lo, :], att.at[2, u, lo, :], dev(dzh=1), R_H + u)
        arrived(att.at[1, u], R_G1 + u)
        send(att.at[1, u, hi, :], att.at[2, u, hi, :], dev(dzh=3), R_H + 4 + u)

    relay(0)
    relay(3)
    relay(1)
    relay(2)
    for d in range(1, NY):
        arrived(wblock, R_WY + d)
    send(wb.at[pl.ds(1, 3), c], wb.at[pl.ds(1, 3), c], dev(dc=1), R_WP)
    arrived(wb.at[pl.ds(1, 3), 1 - c], R_WP)
    project([(3, 0), (3, 1), (3, 2), (3, 3)])
    project([(1, 0), (1, 1), (1, 2), (1, 3)])

    def last(us):
        for u in us:
            arrived(att.at[2, u, lo, :], R_H + u)
            arrived(att.at[2, u, hi, :], R_H + 4 + u)
        project([(2, u) for u in us])

    last((0, 3))
    last((1,))
    last((2,))

    for n, core in ((1, 1 - c), (0, c)):
        mixb[n] = oacc[:, pl.ds(pl.multiple_of(core * FC, FC), FC)].astype(BF)
    send(mixb.at[1], out_ref.at[mine, :], dev(dc=1), R_OUT)
    local(mixb.at[0], out_ref.at[mine, :], R_OL)
    arrived(out_ref.at[mine, :], R_OL)
    arrived(out_ref.at[theirs, :], R_OUT)

    for drain in waits:
        drain()
    for copy in sends:
        copy.wait_send()


N_SEND = 96


def body(queries, keys, values, residual, gate, out_weight):
    projected = pl.pallas_call(
        kernel,
        out_shape=pltpu.VMEM((TOK, FC), BF),
        in_specs=[pl.BlockSpec(memory_space=pltpu.HBM)] * 4,
        out_specs=pl.BlockSpec(memory_space=pltpu.VMEM),
        scratch_shapes=[
            pltpu.VMEM((NX, HALF, HD), BF),
            pltpu.VMEM((2 * NX, 2, TOK, HD), BF),
            pltpu.VMEM((NZH, NX, HALF, HD), BF),
            pltpu.VMEM((NX, HALF, HD), BF),
            pltpu.VMEM((NZH, 2, 256, FEAT), BF),
            pltpu.VMEM((NX, HALF, HD), F32),
            pltpu.VMEM((NX, HALF, 2 * HD), F32),
            pltpu.VMEM((HALF, TOK), F32),
            pltpu.VMEM((HALF, TOK), F32),
            pltpu.VMEM((2, HALF, HD), F32),
            pltpu.VMEM((2, HALF, HD), F32),
            pltpu.VMEM((HALF, FEAT), F32),
            pltpu.VMEM((2, HALF, FC), BF),
            pltpu.SemaphoreType.DMA((N_SEND,)),
            pltpu.SemaphoreType.DMA((N_RECV,)),
        ],
        compiler_params=pltpu.CompilerParams(
            collective_id=0, has_side_effects=True, vmem_limit_bytes=60 * 2**20),
        name="attention",
    )(queries, keys, values, out_weight)
    return (residual.astype(F32) + gate[None, :] * projected.astype(F32)).astype(BF)


def solution(mesh):
    return jax.shard_map(
        body,
        mesh=mesh,
        in_specs=(
            P("ctx", "tp"),
            P("ctx", "tp"),
            P("ctx", "tp"),
            P("ctx", "tp"),
            P("tp"),
            P("tp", None),
        ),
        out_specs=P("ctx", "tp"),
        check_vma=False,
    )
```

```python
import functools
import math

import jax
import jax.numpy as jnp
from jax import lax
from jax.experimental import pallas as pl
from jax.experimental.pallas import tpu as pltpu
from jax.sharding import PartitionSpec as P

MESH = pl.DeviceIdType.MESH
HD = 128
NX, NZL, NY, NZH = 4, 2, 8, 4
TOK = 768
HALF = TOK // 2
FEAT = 768
FC = FEAT // 2
SCALE = math.log2(math.e) / math.sqrt(HD)
BF = jnp.bfloat16
F32 = jnp.float32

R_A, R_B, R_Z, R_Q = 0, 4, 12, 16
R_RET, R_G3, R_G1, R_H = 20, 24, 28, 32
R_WZ, R_WX, R_WY, R_WP, R_WO, R_WL = 40, 44, 48, 56, 57, 58
R_RES, R_GATE, R_RL, R_GL, R_OUT, R_OL = 59, 60, 61, 62, 63, 64
R_AV = 65
N_RECV = 69


def kernel(q_ref, k_ref, v_ref, w_ref, out_ref,
           qb, kv, att, ob, wb, mst, acc, s0, s1, newb, alpb, oacc, mixb, ss, rs):
    ctx = lax.axis_index("ctx")
    tp = lax.axis_index("tp")
    x, zl, y = ctx // (NZL * NY), (ctx // NY) % NZL, ctx % NY
    zh, c = tp // 2, tp % 2

    def dev(dx=0, dzl=0, dy=0, dzh=0, dc=0):
        return ((((x + dx) % NX) * NZL + (zl + dzl) % NZL) * NY + (y + dy) % NY,
                ((zh + dzh) % NZH) * 2 + (c + dc) % 2)

    def dev_abs(xd, r):
        return ((xd * NZL + zl) * NY + y, zh * 2 + r)

    sends = []
    count = [0]

    def send(src, dst, device, recv):
        i = count[0]
        count[0] += 1
        copy = pltpu.make_async_remote_copy(
            src_ref=src, dst_ref=dst, send_sem=ss.at[i], recv_sem=rs.at[recv],
            device_id=device, device_id_type=MESH)
        copy.start()
        sends.append(copy)

    def local(src, dst, recv):
        pltpu.make_async_copy(src, dst, rs.at[recv]).start()

    def arrived(dst, recv):
        pltpu.make_async_copy(dst, dst, rs.at[recv]).wait()

    mine = pl.ds(pl.multiple_of(c * HALF, HALF), HALF)
    theirs = pl.ds(pl.multiple_of((1 - c) * HALF, HALF), HALF)
    wcols = pl.ds(pl.multiple_of(zh * FEAT, FEAT), FEAT)

    local(w_ref.at[:, wcols], wb.at[0, c], R_WL)

    def init(n, _):
        mst[n] = jnp.full((HALF, HD), -1e30, F32)
        acc[n] = jnp.zeros((HALF, 2 * HD), F32)
        return 0

    lax.fori_loop(0, NX, init, 0)

    owner = x // 2 == c
    own_cols = pl.ds(pl.multiple_of((x % 2) * HD, HD), HD)

    @pl.when(owner)
    def _():
        local(k_ref.at[mine, own_cols], kv.at[0, 0, mine, :], R_A)
        local(v_ref.at[mine, own_cols], kv.at[0, 1, mine, :], R_AV)
        local(q_ref.at[mine, own_cols], qb.at[0], R_Q)

    peers = [dev(dx=d, dc=e) for d in (1, 2, 3) for e in (0, 1)]
    peers += [dev(dc=1), dev(dzl=1)]
    peers += [dev(dzh=d) for d in (1, 2, 3)]
    peers += [dev(dy=d) for d in range(1, NY)]
    barrier = pltpu.get_barrier_semaphore()
    for peer in peers:
        pl.semaphore_signal(barrier, inc=1, device_id=peer, device_id_type=MESH)
    pl.semaphore_wait(barrier, len(peers))

    def descriptor(src, dst, device, recv):
        i = count[0]
        count[0] += 1
        copy = pltpu.make_async_remote_copy(
            src_ref=src, dst_ref=dst, send_sem=ss.at[i], recv_sem=rs.at[recv],
            device_id=device, device_id_type=MESH)
        sends.append(copy)
        return copy

    def pass_own(d, n):
        piece = kv.at[d, n, mine, :]
        return [descriptor(piece, kv.at[4 + d, n, mine, :], dev(dzl=1), R_Z + d),
                descriptor(piece, piece, dev(dc=1), R_B + d)]

    own = pass_own(0, 0) + pass_own(0, 1)

    def start_own():
        arrived(kv.at[0, 0, mine, :], R_A)
        arrived(kv.at[0, 1, mine, :], R_AV)
        for copy in own:
            copy.start()

    @pl.when(owner)
    def _():
        start_own()

    wrow = pl.ds(pl.multiple_of(y * 32 + (x % 2) * 16, 16), 16)
    wcol = (x // 2) * FC
    for d in (1, 2, 3):
        zd = (zh + d) % NZH
        send(w_ref.at[wrow, pl.ds(pl.multiple_of(zd * FEAT + wcol, FC), FC)],
             wb.at[4 - d, c, wrow, pl.ds(pl.multiple_of(wcol, FC), FC)],
             dev(dzh=d), R_WZ + 4 - d)

    first = jnp.where((2 * c - x) % NX == 2, 1, 0)
    waits = []

    def exchange(j, when):
        head = (j + first) % 2
        xd = 2 * c + head
        slot = (x - xd) % NX
        cols = pl.ds(pl.multiple_of(head * HD, HD), HD)
        for src, dst, recv in ((k_ref, kv.at[slot, 0], R_A), (v_ref, kv.at[slot, 1], R_AV),
                               (q_ref, qb.at[slot], R_Q)):
            for r in (0, 1):
                rows = pl.ds(r * HALF, HALF)
                i = count[0]
                count[0] += 1
                copy = pltpu.make_async_remote_copy(
                    src_ref=src.at[rows, cols], dst_ref=dst if recv == R_Q else dst.at[rows, :],
                    send_sem=ss.at[i], recv_sem=rs.at[recv + slot],
                    device_id=dev_abs(xd, r), device_id_type=MESH)
                go = jnp.logical_not((xd == x) & (c == r)) & when

                @pl.when(go)
                def _():
                    copy.start()

                def drain(copy=copy, go=go):
                    @pl.when(go)
                    def _():
                        copy.wait_send()

                waits.append(drain)

    far = (x - 2 * c - (1 + first) % 2) % NX == 2
    always = c >= 0
    exchange(0, always)
    exchange(1, jnp.logical_not(far))

    tq = HALF // 2

    def scores(i, s, buf):
        k = kv[s, 0]
        for t in range(HALF // tq):
            rows = pl.ds(t * tq, tq)
            sc = lax.dot_general(qb[i, rows, :], k, (((1,), (1,)), ((), ())),
                                 preferred_element_type=F32)
            (s0, s1)[buf][rows, :] = sc
            old = mst[i, rows, :]
            new = jnp.maximum(old, jnp.max(sc, axis=1, keepdims=True) * SCALE)
            mst[i, rows, :] = new
            newb[buf, rows, :] = new
            alpb[buf, rows, :] = jnp.exp2(old - new)

    def absorb(i, s, buf):
        v = jnp.concatenate([kv[s, 1], jnp.ones((TOK, HD), BF)], axis=1)
        for t in range(HALF // tq):
            rows = pl.ds(t * tq, tq)
            new = newb[buf, rows, :]
            alpha = alpb[buf, rows, :]
            p = jnp.exp2((s0, s1)[buf][rows, :] * SCALE
                         - jnp.concatenate([new] * (TOK // HD), axis=1)).astype(BF)
            pv = jnp.dot(p, v, preferred_element_type=F32)
            acc[i, rows, :] = acc[i, rows, :] * jnp.concatenate([alpha, alpha], axis=1) + pv

    pending = []

    def step(i, s):
        buf = len(pending) % 2
        scores(i, s, buf)
        if pending:
            absorb(*pending[-1], 1 - buf)
        pending.append((i, s))

    def items(pairs):
        for i, n in pairs:
            step(i, n)

    def half_of(s, rows):
        return kv.at[s, :, rows, :]

    def pass_on(d, n):
        arrived(kv.at[d, n, mine, :], (R_A, R_AV)[n] + d)
        for copy in pass_own(d, n):
            copy.start()

    def pass_other(d):
        arrived(half_of(4 + d, mine), R_Z + d)
        send(half_of(4 + d, mine), half_of(4 + d, mine), dev(dc=1), R_B + 4 + d)

    def whole(s):
        arrived(half_of(s, theirs), R_B + s)

    def queries(d):
        arrived(qb.at[d], R_Q + d)

    @pl.when(jnp.logical_not(owner))
    def _():
        start_own()

    send(w_ref.at[:, wcols], wb.at[0, c], dev(dc=1), R_WO)
    queries(0)
    whole(0)
    step(0, 0)
    for d in (1, 2, 3):
        arrived(wb.at[d, c, wrow, pl.ds(pl.multiple_of(wcol, FC), FC)], R_WZ + d)
    wslice = wb.at[pl.ds(1, 3), c, wrow, pl.ds(pl.multiple_of(wcol, FC), FC)]
    for d in (1, 3, 2):
        send(wslice, wslice, dev(dx=d), R_WX + d)
    exchange(1, far)
    pass_on(1, 0)
    pass_on(3, 0)
    pass_on(1, 1)
    pass_on(3, 1)
    pass_other(0)
    whole(1)
    whole(3)
    items([(0, 1), (0, 3)])
    for d in (1, 2, 3):
        arrived(wslice, R_WX + d)
    wblock = wb.at[pl.ds(1, 3), c, pl.ds(pl.multiple_of(y * 32, 32), 32), :]
    for d in (4, 3, 5, 2, 6, 1, 7):
        send(wblock, wblock, dev(dy=d), R_WY + d)
    whole(4)
    queries(1)
    queries(3)
    items([(0, 4), (1, 0), (1, 1), (1, 3), (1, 4), (3, 0)])
    pass_other(1)
    items([(3, 1), (3, 3)])
    pass_on(2, 0)
    pass_on(2, 1)
    whole(5)
    whole(2)
    items([(3, 4), (0, 5), (1, 5), (3, 5), (0, 2), (1, 2)])
    queries(2)
    pass_other(3)
    items([(3, 2), (2, 0), (2, 1), (2, 3), (2, 4), (2, 5)])
    whole(7)
    items([(2, 2), (0, 7)])
    pass_other(2)
    items([(1, 7), (3, 7)])
    step(2, 7)
    whole(6)

    def finish(i):
        ob[i] = (acc[i, :, :HD] / acc[i, :, HD:]).astype(BF)

    def give(i):
        if i == 0:
            send(ob.at[0], att.at[3, 0], dev(dzh=1), R_G3 + 0)
            send(ob.at[0], att.at[1, 0], dev(dzh=3), R_G1 + 0)
        else:
            send(ob.at[i], att.at[0, 4 - i], dev(dx=i), R_RET + 4 - i)

    step(0, 6)
    step(1, 6)
    finish(0)
    step(3, 6)
    finish(1)
    give(0)
    step(2, 6)
    finish(3)
    give(1)
    absorb(*pending[-1], (len(pending) - 1) % 2)
    finish(2)
    give(3)
    att[0, 0] = ob[0]
    give(2)

    ORDER = (0, 3, 1, 2)
    for u in ORDER[1:]:
        arrived(att.at[0, u], R_RET + u)
        send(att.at[0, u], att.at[3, u], dev(dzh=1), R_G3 + u)
        send(att.at[0, u], att.at[1, u], dev(dzh=3), R_G1 + u)

    def wrows(d, u):
        head = (x + u) % NX
        return wb[d, head // 2, pl.ds(pl.multiple_of((head % 2) * HD, HD), HD), :]

    def project(pairs, start=False):
        a = jnp.concatenate([att[d, u] for d, u in pairs], axis=1)
        w = jnp.concatenate([wrows(d, u) for d, u in pairs], axis=0)
        r = jnp.dot(a, w, preferred_element_type=F32)
        oacc[...] = r if start else oacc[...] + r

    arrived(wb.at[0, c], R_WL)
    arrived(wb.at[0, 1 - c], R_WO)
    project([(0, 0), (0, 1), (0, 2), (0, 3)], True)

    lo, hi = pl.ds(0, HALF // 2), pl.ds(HALF // 2, HALF // 2)

    def relay(u):
        arrived(att.at[3, u], R_G3 + u)
        send(att.at[3, u, lo, :], att.at[2, u, lo, :], dev(dzh=1), R_H + u)
        arrived(att.at[1, u], R_G1 + u)
        send(att.at[1, u, hi, :], att.at[2, u, hi, :], dev(dzh=3), R_H + 4 + u)

    relay(0)
    relay(3)
    relay(1)
    relay(2)
    for d in range(1, NY):
        arrived(wblock, R_WY + d)
    send(wb.at[pl.ds(1, 3), c], wb.at[pl.ds(1, 3), c], dev(dc=1), R_WP)
    arrived(wb.at[pl.ds(1, 3), 1 - c], R_WP)
    project([(3, 0), (3, 1), (3, 2), (3, 3)])
    project([(1, 0), (1, 1), (1, 2), (1, 3)])

    def last(us):
        for u in us:
            arrived(att.at[2, u, lo, :], R_H + u)
            arrived(att.at[2, u, hi, :], R_H + 4 + u)
        project([(2, u) for u in us])

    last((0, 3))
    last((1,))
    arrived(att.at[2, 2, lo, :], R_H + 2)
    arrived(att.at[2, 2, hi, :], R_H + 4 + 2)
    head = (x + 2) % NX
    for n, core in ((1, 1 - c), (0, c)):
        cols = pl.ds(pl.multiple_of(core * FC, FC), FC)
        w = wb[2, head // 2, pl.ds(pl.multiple_of((head % 2) * HD, HD), HD), cols]
        mixb[n] = (oacc[:, cols] + jnp.dot(att[2, 2], w, preferred_element_type=F32)).astype(BF)
    send(mixb.at[1], out_ref.at[mine, :], dev(dc=1), R_OUT)
    local(mixb.at[0], out_ref.at[mine, :], R_OL)
    arrived(out_ref.at[mine, :], R_OL)
    arrived(out_ref.at[theirs, :], R_OUT)

    for drain in waits:
        drain()
    for copy in sends:
        copy.wait_send()


N_SEND = 96


def body(queries, keys, values, residual, gate, out_weight):
    projected = pl.pallas_call(
        kernel,
        out_shape=pltpu.VMEM((TOK, FC), BF),
        in_specs=[pl.BlockSpec(memory_space=pltpu.HBM)] * 4,
        out_specs=pl.BlockSpec(memory_space=pltpu.VMEM),
        scratch_shapes=[
            pltpu.VMEM((NX, HALF, HD), BF),
            pltpu.VMEM((2 * NX, 2, TOK, HD), BF),
            pltpu.VMEM((NZH, NX, HALF, HD), BF),
            pltpu.VMEM((NX, HALF, HD), BF),
            pltpu.VMEM((NZH, 2, 256, FEAT), BF),
            pltpu.VMEM((NX, HALF, HD), F32),
            pltpu.VMEM((NX, HALF, 2 * HD), F32),
            pltpu.VMEM((HALF, TOK), F32),
            pltpu.VMEM((HALF, TOK), F32),
            pltpu.VMEM((2, HALF, HD), F32),
            pltpu.VMEM((2, HALF, HD), F32),
            pltpu.VMEM((HALF, FEAT), F32),
            pltpu.VMEM((2, HALF, FC), BF),
            pltpu.SemaphoreType.DMA((N_SEND,)),
            pltpu.SemaphoreType.DMA((N_RECV,)),
        ],
        compiler_params=pltpu.CompilerParams(
            collective_id=0, has_side_effects=True, vmem_limit_bytes=60 * 2**20),
        name="attention",
    )(queries, keys, values, out_weight)
    return (residual.astype(F32) + gate[None, :] * projected.astype(F32)).astype(BF)


def solution(mesh):
    return jax.shard_map(
        body,
        mesh=mesh,
        in_specs=(
            P("ctx", "tp"),
            P("ctx", "tp"),
            P("ctx", "tp"),
            P("ctx", "tp"),
            P("tp"),
            P("tp", None),
        ),
        out_specs=P("ctx", "tp"),
        check_vma=False,
    )
```

```python
import functools
import math

import jax
import jax.numpy as jnp
from jax import lax
from jax.experimental import pallas as pl
from jax.experimental.pallas import tpu as pltpu
from jax.sharding import PartitionSpec as P

MESH = pl.DeviceIdType.MESH
HD = 128
NX, NZL, NY, NZH = 4, 2, 8, 4
TOK = 768
HALF = TOK // 2
FEAT = 768
FC = FEAT // 2
SCALE = math.log2(math.e) / math.sqrt(HD)
BF = jnp.bfloat16
F32 = jnp.float32

R_A, R_B, R_Z, R_Q = 0, 4, 12, 16
R_RET, R_G3, R_G1, R_H = 20, 24, 28, 32
R_WZ, R_WX, R_WP, R_WO, R_WL = 40, 44, 56, 57, 58
R_RES, R_GATE, R_RL, R_GL, R_OUT, R_OL = 59, 60, 61, 62, 63, 64
R_AV = 65
N_RECV = 69


def kernel(q_ref, k_ref, v_ref, w_ref, out_ref,
           qb, kv, att, ob, wb, mst, acc, s0, s1, newb, alpb, oacc, mixb, ss, rs):
    ctx = lax.axis_index("ctx")
    tp = lax.axis_index("tp")
    x, zl, y = ctx // (NZL * NY), (ctx // NY) % NZL, ctx % NY
    zh, c = tp // 2, tp % 2

    def dev(dx=0, dzl=0, dy=0, dzh=0, dc=0):
        return ((((x + dx) % NX) * NZL + (zl + dzl) % NZL) * NY + (y + dy) % NY,
                ((zh + dzh) % NZH) * 2 + (c + dc) % 2)

    def dev_abs(xd, r):
        return ((xd * NZL + zl) * NY + y, zh * 2 + r)

    sends = []
    count = [0]

    def send(src, dst, device, recv):
        i = count[0]
        count[0] += 1
        copy = pltpu.make_async_remote_copy(
            src_ref=src, dst_ref=dst, send_sem=ss.at[i], recv_sem=rs.at[recv],
            device_id=device, device_id_type=MESH)
        copy.start()
        sends.append(copy)

    def local(src, dst, recv):
        pltpu.make_async_copy(src, dst, rs.at[recv]).start()

    def arrived(dst, recv):
        pltpu.make_async_copy(dst, dst, rs.at[recv]).wait()

    mine = pl.ds(pl.multiple_of(c * HALF, HALF), HALF)
    theirs = pl.ds(pl.multiple_of((1 - c) * HALF, HALF), HALF)
    wcols = pl.ds(pl.multiple_of(zh * FEAT, FEAT), FEAT)

    local(w_ref.at[:, wcols], wb.at[0, c], R_WL)

    def init(n, _):
        mst[n] = jnp.full((HALF, HD), -1e30, F32)
        acc[n] = jnp.zeros((HALF, 2 * HD), F32)
        return 0

    lax.fori_loop(0, NX, init, 0)

    owner = x // 2 == c
    own_cols = pl.ds(pl.multiple_of((x % 2) * HD, HD), HD)

    @pl.when(owner)
    def _():
        local(k_ref.at[mine, own_cols], kv.at[0, 0, mine, :], R_A)
        local(v_ref.at[mine, own_cols], kv.at[0, 1, mine, :], R_AV)
        local(q_ref.at[mine, own_cols], qb.at[0], R_Q)

    peers = [dev(dx=d, dc=e) for d in (1, 2, 3) for e in (0, 1)]
    peers += [dev(dc=1), dev(dzl=1)]
    peers += [dev(dzh=d) for d in (1, 2, 3)]
    barrier = pltpu.get_barrier_semaphore()
    for peer in peers:
        pl.semaphore_signal(barrier, inc=1, device_id=peer, device_id_type=MESH)
    pl.semaphore_wait(barrier, len(peers))

    def descriptor(src, dst, device, recv):
        i = count[0]
        count[0] += 1
        copy = pltpu.make_async_remote_copy(
            src_ref=src, dst_ref=dst, send_sem=ss.at[i], recv_sem=rs.at[recv],
            device_id=device, device_id_type=MESH)
        sends.append(copy)
        return copy

    def pass_own(d, n):
        piece = kv.at[d, n, mine, :]
        return [descriptor(piece, kv.at[4 + d, n, mine, :], dev(dzl=1), R_Z + d),
                descriptor(piece, piece, dev(dc=1), R_B + d)]

    own = pass_own(0, 0) + pass_own(0, 1)

    def start_own():
        arrived(kv.at[0, 0, mine, :], R_A)
        arrived(kv.at[0, 1, mine, :], R_AV)
        for copy in own:
            copy.start()

    @pl.when(owner)
    def _():
        start_own()

    wrow = pl.ds(pl.multiple_of((x % 2) * HD, HD), HD)
    wcol = (x // 2) * FC
    wslice = wb.at[pl.ds(1, 3), c, wrow, pl.ds(pl.multiple_of(wcol, FC), FC)]

    def weights_z():
        for d in (1, 3, 2):
            zd = (zh + d) % NZH
            send(w_ref.at[wrow, pl.ds(pl.multiple_of(zd * FEAT + wcol, FC), FC)],
                 wb.at[4 - d, c, wrow, pl.ds(pl.multiple_of(wcol, FC), FC)],
                 dev(dzh=d), R_WZ + 4 - d)

    def weights_x():
        for d in (1, 2, 3):
            arrived(wb.at[d, c, wrow, pl.ds(pl.multiple_of(wcol, FC), FC)], R_WZ + d)
        for d in (1, 3, 2):
            send(wslice, wslice, dev(dx=d), R_WX + d)

    def weights_core():
        for d in (1, 2, 3):
            arrived(wslice, R_WX + d)
        send(wb.at[pl.ds(1, 3), c], wb.at[pl.ds(1, 3), c], dev(dc=1), R_WP)

    first = jnp.where((2 * c - x) % NX == 2, 1, 0)
    waits = []

    def exchange(j, when):
        head = (j + first) % 2
        xd = 2 * c + head
        slot = (x - xd) % NX
        cols = pl.ds(pl.multiple_of(head * HD, HD), HD)
        for src, dst, recv in ((k_ref, kv.at[slot, 0], R_A), (v_ref, kv.at[slot, 1], R_AV),
                               (q_ref, qb.at[slot], R_Q)):
            for r in (0, 1):
                rows = pl.ds(r * HALF, HALF)
                i = count[0]
                count[0] += 1
                copy = pltpu.make_async_remote_copy(
                    src_ref=src.at[rows, cols], dst_ref=dst if recv == R_Q else dst.at[rows, :],
                    send_sem=ss.at[i], recv_sem=rs.at[recv + slot],
                    device_id=dev_abs(xd, r), device_id_type=MESH)
                go = jnp.logical_not((xd == x) & (c == r)) & when

                @pl.when(go)
                def _():
                    copy.start()

                def drain(copy=copy, go=go):
                    @pl.when(go)
                    def _():
                        copy.wait_send()

                waits.append(drain)

    always = c >= 0
    exchange(0, always)
    exchange(1, always)

    tq = HALF // 2

    def scores(i, s, buf):
        k = kv[s, 0]
        for t in range(HALF // tq):
            rows = pl.ds(t * tq, tq)
            sc = lax.dot_general(qb[i, rows, :], k, (((1,), (1,)), ((), ())),
                                 preferred_element_type=F32)
            (s0, s1)[buf][rows, :] = sc
            old = mst[i, rows, :]
            new = jnp.maximum(old, jnp.max(sc, axis=1, keepdims=True) * SCALE)
            mst[i, rows, :] = new
            newb[buf, rows, :] = new
            alpb[buf, rows, :] = jnp.exp2(old - new)

    def absorb(i, s, buf):
        v = jnp.concatenate([kv[s, 1], jnp.ones((TOK, HD), BF)], axis=1)
        for t in range(HALF // tq):
            rows = pl.ds(t * tq, tq)
            new = newb[buf, rows, :]
            alpha = alpb[buf, rows, :]
            p = jnp.exp2((s0, s1)[buf][rows, :] * SCALE
                         - jnp.concatenate([new] * (TOK // HD), axis=1)).astype(BF)
            pv = jnp.dot(p, v, preferred_element_type=F32)
            acc[i, rows, :] = acc[i, rows, :] * jnp.concatenate([alpha, alpha], axis=1) + pv

    pending = []

    def step(i, s):
        buf = len(pending) % 2
        scores(i, s, buf)
        if pending:
            absorb(*pending[-1], 1 - buf)
        pending.append((i, s))

    def items(pairs):
        for i, n in pairs:
            step(i, n)

    def half_of(s, rows):
        return kv.at[s, :, rows, :]

    def pass_on(d, n):
        arrived(kv.at[d, n, mine, :], (R_A, R_AV)[n] + d)
        for copy in pass_own(d, n):
            copy.start()

    def pass_other(d):
        arrived(half_of(4 + d, mine), R_Z + d)
        send(half_of(4 + d, mine), half_of(4 + d, mine), dev(dc=1), R_B + 4 + d)

    def whole(s):
        arrived(half_of(s, theirs), R_B + s)

    def queries(d):
        arrived(qb.at[d], R_Q + d)

    @pl.when(jnp.logical_not(owner))
    def _():
        start_own()

    send(w_ref.at[:, wcols], wb.at[0, c], dev(dc=1), R_WO)
    queries(0)
    whole(0)
    step(0, 0)
    pass_on(1, 0)
    pass_on(3, 0)
    pass_on(1, 1)
    pass_on(3, 1)
    pass_other(0)
    whole(1)
    whole(3)
    items([(0, 1), (0, 3)])
    whole(4)
    queries(1)
    queries(3)
    items([(0, 4), (1, 0), (1, 1), (1, 3), (1, 4), (3, 0)])
    pass_other(1)
    items([(3, 1), (3, 3)])
    pass_on(2, 0)
    pass_on(2, 1)
    whole(5)
    whole(2)
    items([(3, 4), (0, 5), (1, 5), (3, 5), (0, 2), (1, 2)])
    queries(2)
    pass_other(3)
    weights_z()
    items([(3, 2), (2, 0), (2, 1), (2, 3), (2, 4), (2, 5)])
    whole(7)
    items([(2, 2), (0, 7)])
    pass_other(2)
    items([(1, 7), (3, 7)])
    step(2, 7)
    whole(6)

    def finish(i):
        ob[i] = (acc[i, :, :HD] / acc[i, :, HD:]).astype(BF)

    def give(i):
        if i == 0:
            send(ob.at[0], att.at[3, 0], dev(dzh=1), R_G3 + 0)
            send(ob.at[0], att.at[1, 0], dev(dzh=3), R_G1 + 0)
        else:
            send(ob.at[i], att.at[0, 4 - i], dev(dx=i), R_RET + 4 - i)

    step(0, 6)
    step(1, 6)
    finish(0)
    step(3, 6)
    finish(1)
    give(0)
    step(2, 6)
    finish(3)
    give(1)
    absorb(*pending[-1], (len(pending) - 1) % 2)
    finish(2)
    give(3)
    att[0, 0] = ob[0]
    give(2)

    ORDER = (0, 3, 1, 2)
    for u in ORDER[1:]:
        arrived(att.at[0, u], R_RET + u)
        send(att.at[0, u], att.at[3, u], dev(dzh=1), R_G3 + u)
        send(att.at[0, u], att.at[1, u], dev(dzh=3), R_G1 + u)
        if u == 3:
            weights_x()

    def wrows(d, u):
        head = (x + u) % NX
        return wb[d, head // 2, pl.ds(pl.multiple_of((head % 2) * HD, HD), HD), :]

    def project(pairs, start=False):
        a = jnp.concatenate([att[d, u] for d, u in pairs], axis=1)
        w = jnp.concatenate([wrows(d, u) for d, u in pairs], axis=0)
        r = jnp.dot(a, w, preferred_element_type=F32)
        oacc[...] = r if start else oacc[...] + r

    arrived(wb.at[0, c], R_WL)
    arrived(wb.at[0, 1 - c], R_WO)
    project([(0, 0), (0, 1), (0, 2), (0, 3)], True)

    lo, hi = pl.ds(0, HALF // 2), pl.ds(HALF // 2, HALF // 2)

    def relay(u):
        arrived(att.at[3, u], R_G3 + u)
        send(att.at[3, u, lo, :], att.at[2, u, lo, :], dev(dzh=1), R_H + u)
        arrived(att.at[1, u], R_G1 + u)
        send(att.at[1, u, hi, :], att.at[2, u, hi, :], dev(dzh=3), R_H + 4 + u)

    relay(0)
    relay(3)
    relay(1)
    relay(2)
    weights_core()
    arrived(wb.at[pl.ds(1, 3), 1 - c], R_WP)
    project([(3, 0), (3, 1), (3, 2), (3, 3)])
    project([(1, 0), (1, 1), (1, 2), (1, 3)])

    def last(us):
        for u in us:
            arrived(att.at[2, u, lo, :], R_H + u)
            arrived(att.at[2, u, hi, :], R_H + 4 + u)
        project([(2, u) for u in us])

    last((0, 3))
    last((1,))
    arrived(att.at[2, 2, lo, :], R_H + 2)
    arrived(att.at[2, 2, hi, :], R_H + 4 + 2)
    head = (x + 2) % NX
    for n, core in ((1, 1 - c), (0, c)):
        cols = pl.ds(pl.multiple_of(core * FC, FC), FC)
        w = wb[2, head // 2, pl.ds(pl.multiple_of((head % 2) * HD, HD), HD), cols]
        mixb[n] = (oacc[:, cols] + jnp.dot(att[2, 2], w, preferred_element_type=F32)).astype(BF)
    send(mixb.at[1], out_ref.at[mine, :], dev(dc=1), R_OUT)
    local(mixb.at[0], out_ref.at[mine, :], R_OL)
    arrived(out_ref.at[mine, :], R_OL)
    arrived(out_ref.at[theirs, :], R_OUT)

    for drain in waits:
        drain()
    for copy in sends:
        copy.wait_send()


N_SEND = 96


def body(queries, keys, values, residual, gate, out_weight):
    projected = pl.pallas_call(
        kernel,
        out_shape=pltpu.VMEM((TOK, FC), BF),
        in_specs=[pl.BlockSpec(memory_space=pltpu.HBM)] * 4,
        out_specs=pl.BlockSpec(memory_space=pltpu.VMEM),
        scratch_shapes=[
            pltpu.VMEM((NX, HALF, HD), BF),
            pltpu.VMEM((2 * NX, 2, TOK, HD), BF),
            pltpu.VMEM((NZH, NX, HALF, HD), BF),
            pltpu.VMEM((NX, HALF, HD), BF),
            pltpu.VMEM((NZH, 2, 256, FEAT), BF),
            pltpu.VMEM((NX, HALF, HD), F32),
            pltpu.VMEM((NX, HALF, 2 * HD), F32),
            pltpu.VMEM((HALF, TOK), F32),
            pltpu.VMEM((HALF, TOK), F32),
            pltpu.VMEM((2, HALF, HD), F32),
            pltpu.VMEM((2, HALF, HD), F32),
            pltpu.VMEM((HALF, FEAT), F32),
            pltpu.VMEM((2, HALF, FC), BF),
            pltpu.SemaphoreType.DMA((N_SEND,)),
            pltpu.SemaphoreType.DMA((N_RECV,)),
        ],
        compiler_params=pltpu.CompilerParams(
            collective_id=0, has_side_effects=True, vmem_limit_bytes=60 * 2**20),
        name="attention",
    )(queries, keys, values, out_weight)
    return (residual.astype(F32) + gate[None, :] * projected.astype(F32)).astype(BF)


def solution(mesh):
    return jax.shard_map(
        body,
        mesh=mesh,
        in_specs=(
            P("ctx", "tp"),
            P("ctx", "tp"),
            P("ctx", "tp"),
            P("ctx", "tp"),
            P("tp"),
            P("tp", None),
        ),
        out_specs=P("ctx", "tp"),
        check_vma=False,
    )
```

```python
import functools
import math

import jax
import jax.numpy as jnp
from jax import lax
from jax.experimental import pallas as pl
from jax.experimental.pallas import tpu as pltpu
from jax.sharding import PartitionSpec as P

MESH = pl.DeviceIdType.MESH
HD = 128
NX, NZL, NY, NZH = 4, 2, 8, 4
TOK = 768
HALF = TOK // 2
FEAT = 768
FC = FEAT // 2
SCALE = math.log2(math.e) / math.sqrt(HD)
BF = jnp.bfloat16
F32 = jnp.float32

R_A, R_B, R_Z, R_Q = 0, 4, 12, 16
R_RET, R_G3, R_G1, R_H = 20, 24, 28, 32
R_WZ, R_WX, R_WP, R_WO, R_WL = 40, 44, 56, 57, 58
R_RES, R_GATE, R_RL, R_GL, R_OUT, R_OL = 59, 60, 61, 62, 63, 64
R_AV, R_WR, R_W2 = 65, 69, 71
N_RECV = 73


def kernel(q_ref, k_ref, v_ref, w_ref, out_ref,
           qb, kv, att, ob, wb, wpass, mst, acc, s0, s1, newb, alpb, oacc, mixb, ss, rs):
    ctx = lax.axis_index("ctx")
    tp = lax.axis_index("tp")
    x, zl, y = ctx // (NZL * NY), (ctx // NY) % NZL, ctx % NY
    zh, c = tp // 2, tp % 2

    def dev(dx=0, dzl=0, dy=0, dzh=0, dc=0):
        return ((((x + dx) % NX) * NZL + (zl + dzl) % NZL) * NY + (y + dy) % NY,
                ((zh + dzh) % NZH) * 2 + (c + dc) % 2)

    def dev_abs(xd, r):
        return ((xd * NZL + zl) * NY + y, zh * 2 + r)

    sends = []
    count = [0]

    def send(src, dst, device, recv):
        i = count[0]
        count[0] += 1
        copy = pltpu.make_async_remote_copy(
            src_ref=src, dst_ref=dst, send_sem=ss.at[i], recv_sem=rs.at[recv],
            device_id=device, device_id_type=MESH)
        copy.start()
        sends.append(copy)

    def local(src, dst, recv):
        pltpu.make_async_copy(src, dst, rs.at[recv]).start()

    def arrived(dst, recv):
        pltpu.make_async_copy(dst, dst, rs.at[recv]).wait()

    mine = pl.ds(pl.multiple_of(c * HALF, HALF), HALF)
    theirs = pl.ds(pl.multiple_of((1 - c) * HALF, HALF), HALF)
    wcols = pl.ds(pl.multiple_of(zh * FEAT, FEAT), FEAT)

    local(w_ref.at[:, wcols], wb.at[0, c], R_WL)

    def init(n, _):
        mst[n] = jnp.full((HALF, HD), -1e30, F32)
        acc[n] = jnp.zeros((HALF, 2 * HD), F32)
        return 0

    lax.fori_loop(0, NX, init, 0)

    owner = x // 2 == c
    own_cols = pl.ds(pl.multiple_of((x % 2) * HD, HD), HD)

    @pl.when(owner)
    def _():
        local(k_ref.at[mine, own_cols], kv.at[0, 0, mine, :], R_A)
        local(v_ref.at[mine, own_cols], kv.at[0, 1, mine, :], R_AV)
        local(q_ref.at[mine, own_cols], qb.at[0], R_Q)

    peers = [dev(dx=d, dc=e) for d in (1, 2, 3) for e in (0, 1)]
    peers += [dev(dc=1), dev(dzl=1)]
    peers += [dev(dzh=d) for d in (1, 3)]
    barrier = pltpu.get_barrier_semaphore()
    for peer in peers:
        pl.semaphore_signal(barrier, inc=1, device_id=peer, device_id_type=MESH)
    pl.semaphore_wait(barrier, len(peers))

    def descriptor(src, dst, device, recv):
        i = count[0]
        count[0] += 1
        copy = pltpu.make_async_remote_copy(
            src_ref=src, dst_ref=dst, send_sem=ss.at[i], recv_sem=rs.at[recv],
            device_id=device, device_id_type=MESH)
        sends.append(copy)
        return copy

    def pass_own(d, n):
        piece = kv.at[d, n, mine, :]
        return [descriptor(piece, kv.at[4 + d, n, mine, :], dev(dzl=1), R_Z + d),
                descriptor(piece, piece, dev(dc=1), R_B + d)]

    own = pass_own(0, 0) + pass_own(0, 1)

    def start_own():
        arrived(kv.at[0, 0, mine, :], R_A)
        arrived(kv.at[0, 1, mine, :], R_AV)
        for copy in own:
            copy.start()

    @pl.when(owner)
    def _():
        start_own()

    wrow = pl.ds(pl.multiple_of((x % 2) * HD, HD), HD)
    wcol = (x // 2) * FC
    wslice = wb.at[pl.ds(1, 3), c, wrow, pl.ds(pl.multiple_of(wcol, FC), FC)]

    wpart = [pl.ds(pl.multiple_of((x % 2) * HD + n * (HD // 2), HD // 2), HD // 2) for n in (0, 1)]
    wcs = pl.ds(pl.multiple_of(wcol, FC), FC)

    def weights_z():
        for d in (1, 3):
            zd = (zh + d) % NZH
            send(w_ref.at[wrow, pl.ds(pl.multiple_of(zd * FEAT + wcol, FC), FC)],
                 wb.at[4 - d, c, wrow, wcs], dev(dzh=d), R_WZ + 4 - d)
        zd = (zh + 2) % NZH
        for n, d in ((0, 1), (1, 3)):
            send(w_ref.at[wpart[n], pl.ds(pl.multiple_of(zd * FEAT + wcol, FC), FC)],
                 wpass.at[n], dev(dzh=d), R_WR + n)

    def weights_pass():
        for n, d in ((0, 1), (1, 3)):
            arrived(wpass.at[n], R_WR + n)
            send(wpass.at[n], wb.at[2, c, wpart[n], wcs], dev(dzh=d), R_W2 + n)

    def weights_x(blocks):
        for b in blocks:
            if b == 2:
                for n in (0, 1):
                    arrived(wb.at[2, c, wpart[n], wcs], R_W2 + n)
            else:
                arrived(wb.at[b, c, wrow, wcs], R_WZ + b)
        for d in (1, 3, 2):
            for b in blocks:
                send(wb.at[b, c, wrow, wcs], wb.at[b, c, wrow, wcs], dev(dx=d), R_WX + d)

    def weights_core():
        for d in (1, 2, 3):
            arrived(wslice, R_WX + d)
        send(wb.at[pl.ds(1, 3), c], wb.at[pl.ds(1, 3), c], dev(dc=1), R_WP)

    first = jnp.where((2 * c - x) % NX == 2, 1, 0)
    waits = []

    def exchange(j, when):
        head = (j + first) % 2
        xd = 2 * c + head
        slot = (x - xd) % NX
        cols = pl.ds(pl.multiple_of(head * HD, HD), HD)
        for src, dst, recv in ((k_ref, kv.at[slot, 0], R_A), (v_ref, kv.at[slot, 1], R_AV),
                               (q_ref, qb.at[slot], R_Q)):
            for r in (0, 1):
                rows = pl.ds(r * HALF, HALF)
                i = count[0]
                count[0] += 1
                copy = pltpu.make_async_remote_copy(
                    src_ref=src.at[rows, cols], dst_ref=dst if recv == R_Q else dst.at[rows, :],
                    send_sem=ss.at[i], recv_sem=rs.at[recv + slot],
                    device_id=dev_abs(xd, r), device_id_type=MESH)
                go = jnp.logical_not((xd == x) & (c == r)) & when

                @pl.when(go)
                def _():
                    copy.start()

                def drain(copy=copy, go=go):
                    @pl.when(go)
                    def _():
                        copy.wait_send()

                waits.append(drain)

    always = c >= 0
    exchange(0, always)
    exchange(1, always)

    tq = HALF // 2

    def scores(i, s, buf):
        k = kv[s, 0]
        for t in range(HALF // tq):
            rows = pl.ds(t * tq, tq)
            sc = lax.dot_general(qb[i, rows, :], k, (((1,), (1,)), ((), ())),
                                 preferred_element_type=F32)
            (s0, s1)[buf][rows, :] = sc
            old = mst[i, rows, :]
            new = jnp.maximum(old, jnp.max(sc, axis=1, keepdims=True) * SCALE)
            mst[i, rows, :] = new
            newb[buf, rows, :] = new
            alpb[buf, rows, :] = jnp.exp2(old - new)

    def absorb(i, s, buf):
        v = jnp.concatenate([kv[s, 1], jnp.ones((TOK, HD), BF)], axis=1)
        for t in range(HALF // tq):
            rows = pl.ds(t * tq, tq)
            new = newb[buf, rows, :]
            alpha = alpb[buf, rows, :]
            p = jnp.exp2((s0, s1)[buf][rows, :] * SCALE
                         - jnp.concatenate([new] * (TOK // HD), axis=1)).astype(BF)
            pv = jnp.dot(p, v, preferred_element_type=F32)
            acc[i, rows, :] = acc[i, rows, :] * jnp.concatenate([alpha, alpha], axis=1) + pv

    pending = []

    def step(i, s):
        buf = len(pending) % 2
        scores(i, s, buf)
        if pending:
            absorb(*pending[-1], 1 - buf)
        pending.append((i, s))

    def items(pairs):
        for i, n in pairs:
            step(i, n)

    def half_of(s, rows):
        return kv.at[s, :, rows, :]

    def pass_on(d, n):
        arrived(kv.at[d, n, mine, :], (R_A, R_AV)[n] + d)
        for copy in pass_own(d, n):
            copy.start()

    def pass_other(d):
        arrived(half_of(4 + d, mine), R_Z + d)
        send(half_of(4 + d, mine), half_of(4 + d, mine), dev(dc=1), R_B + 4 + d)

    def whole(s):
        arrived(half_of(s, theirs), R_B + s)

    def queries(d):
        arrived(qb.at[d], R_Q + d)

    @pl.when(jnp.logical_not(owner))
    def _():
        start_own()

    send(w_ref.at[:, wcols], wb.at[0, c], dev(dc=1), R_WO)
    queries(0)
    whole(0)
    step(0, 0)
    pass_on(1, 0)
    pass_on(3, 0)
    pass_on(1, 1)
    pass_on(3, 1)
    pass_other(0)
    whole(1)
    whole(3)
    items([(0, 1), (0, 3)])
    whole(4)
    queries(1)
    queries(3)
    items([(0, 4), (1, 0), (1, 1), (1, 3), (1, 4), (3, 0)])
    pass_other(1)
    items([(3, 1), (3, 3)])
    pass_on(2, 0)
    pass_on(2, 1)
    whole(5)
    whole(2)
    items([(3, 4), (0, 5), (1, 5), (3, 5), (0, 2), (1, 2)])
    queries(2)
    pass_other(3)
    weights_z()
    items([(3, 2), (2, 0), (2, 1), (2, 3), (2, 4), (2, 5)])
    whole(7)
    items([(2, 2), (0, 7)])
    pass_other(2)
    items([(1, 7), (3, 7)])
    step(2, 7)
    whole(6)

    def finish(i):
        ob[i] = (acc[i, :, :HD] / acc[i, :, HD:]).astype(BF)

    def give(i):
        if i == 0:
            send(ob.at[0], att.at[3, 0], dev(dzh=1), R_G3 + 0)
            send(ob.at[0], att.at[1, 0], dev(dzh=3), R_G1 + 0)
        else:
            send(ob.at[i], att.at[0, 4 - i], dev(dx=i), R_RET + 4 - i)

    step(0, 6)
    step(1, 6)
    finish(0)
    step(3, 6)
    finish(1)
    give(0)
    step(2, 6)
    finish(3)
    give(1)
    absorb(*pending[-1], (len(pending) - 1) % 2)
    finish(2)
    give(3)
    att[0, 0] = ob[0]
    give(2)
    weights_pass()

    ORDER = (0, 3, 1, 2)
    for u in ORDER[1:]:
        arrived(att.at[0, u], R_RET + u)
        send(att.at[0, u], att.at[3, u], dev(dzh=1), R_G3 + u)
        send(att.at[0, u], att.at[1, u], dev(dzh=3), R_G1 + u)
        if u == 3:
            weights_x((1, 3))

    def wrows(d, u):
        head = (x + u) % NX
        return wb[d, head // 2, pl.ds(pl.multiple_of((head % 2) * HD, HD), HD), :]

    def project(pairs, start=False):
        a = jnp.concatenate([att[d, u] for d, u in pairs], axis=1)
        w = jnp.concatenate([wrows(d, u) for d, u in pairs], axis=0)
        r = jnp.dot(a, w, preferred_element_type=F32)
        oacc[...] = r if start else oacc[...] + r

    arrived(wb.at[0, c], R_WL)
    arrived(wb.at[0, 1 - c], R_WO)
    project([(0, 0), (0, 1), (0, 2), (0, 3)], True)

    lo, hi = pl.ds(0, HALF // 2), pl.ds(HALF // 2, HALF // 2)

    def relay(u):
        arrived(att.at[3, u], R_G3 + u)
        send(att.at[3, u, lo, :], att.at[2, u, lo, :], dev(dzh=1), R_H + u)
        arrived(att.at[1, u], R_G1 + u)
        send(att.at[1, u, hi, :], att.at[2, u, hi, :], dev(dzh=3), R_H + 4 + u)

    relay(0)
    relay(3)
    weights_x((2,))
    relay(1)
    relay(2)
    weights_core()
    arrived(wb.at[pl.ds(1, 3), 1 - c], R_WP)
    project([(3, 0), (3, 1), (3, 2), (3, 3)])
    project([(1, 0), (1, 1), (1, 2), (1, 3)])

    def last(us):
        for u in us:
            arrived(att.at[2, u, lo, :], R_H + u)
            arrived(att.at[2, u, hi, :], R_H + 4 + u)
        project([(2, u) for u in us])

    last((0, 3))
    last((1,))
    arrived(att.at[2, 2, lo, :], R_H + 2)
    arrived(att.at[2, 2, hi, :], R_H + 4 + 2)
    head = (x + 2) % NX
    for n, core in ((1, 1 - c), (0, c)):
        cols = pl.ds(pl.multiple_of(core * FC, FC), FC)
        w = wb[2, head // 2, pl.ds(pl.multiple_of((head % 2) * HD, HD), HD), cols]
        mixb[n] = (oacc[:, cols] + jnp.dot(att[2, 2], w, preferred_element_type=F32)).astype(BF)
    send(mixb.at[1], out_ref.at[mine, :], dev(dc=1), R_OUT)
    local(mixb.at[0], out_ref.at[mine, :], R_OL)
    arrived(out_ref.at[mine, :], R_OL)
    arrived(out_ref.at[theirs, :], R_OUT)

    for drain in waits:
        drain()
    for copy in sends:
        copy.wait_send()


N_SEND = 96


def body(queries, keys, values, residual, gate, out_weight):
    projected = pl.pallas_call(
        kernel,
        out_shape=pltpu.VMEM((TOK, FC), BF),
        in_specs=[pl.BlockSpec(memory_space=pltpu.HBM)] * 4,
        out_specs=pl.BlockSpec(memory_space=pltpu.VMEM),
        scratch_shapes=[
            pltpu.VMEM((NX, HALF, HD), BF),
            pltpu.VMEM((2 * NX, 2, TOK, HD), BF),
            pltpu.VMEM((NZH, NX, HALF, HD), BF),
            pltpu.VMEM((NX, HALF, HD), BF),
            pltpu.VMEM((NZH, 2, 256, FEAT), BF),
            pltpu.VMEM((2, HD // 2, FC), BF),
            pltpu.VMEM((NX, HALF, HD), F32),
            pltpu.VMEM((NX, HALF, 2 * HD), F32),
            pltpu.VMEM((HALF, TOK), F32),
            pltpu.VMEM((HALF, TOK), F32),
            pltpu.VMEM((2, HALF, HD), F32),
            pltpu.VMEM((2, HALF, HD), F32),
            pltpu.VMEM((HALF, FEAT), F32),
            pltpu.VMEM((2, HALF, FC), BF),
            pltpu.SemaphoreType.DMA((N_SEND,)),
            pltpu.SemaphoreType.DMA((N_RECV,)),
        ],
        compiler_params=pltpu.CompilerParams(
            collective_id=0, has_side_effects=True, vmem_limit_bytes=60 * 2**20),
        name="attention",
    )(queries, keys, values, out_weight)
    return (residual.astype(F32) + gate[None, :] * projected.astype(F32)).astype(BF)


def solution(mesh):
    return jax.shard_map(
        body,
        mesh=mesh,
        in_specs=(
            P("ctx", "tp"),
            P("ctx", "tp"),
            P("ctx", "tp"),
            P("ctx", "tp"),
            P("tp"),
            P("tp", None),
        ),
        out_specs=P("ctx", "tp"),
        check_vma=False,
    )
```

```python
import functools
import math

import jax
import jax.numpy as jnp
from jax import lax
from jax.experimental import pallas as pl
from jax.experimental.pallas import tpu as pltpu
from jax.sharding import PartitionSpec as P

MESH = pl.DeviceIdType.MESH
HD = 128
NX, NZL, NY, NZH = 4, 2, 8, 4
TOK = 768
HALF = TOK // 2
FEAT = 768
FC = FEAT // 2
SCALE = math.log2(math.e) / math.sqrt(HD)
BF = jnp.bfloat16
F32 = jnp.float32

R_A, R_B, R_Z, R_Q = 0, 4, 12, 16
R_RET, R_G3, R_G1, R_H = 20, 24, 28, 32
R_WZ, R_WX, R_WP, R_WO, R_WL = 40, 44, 56, 57, 58
R_RES, R_GATE, R_RL, R_GL, R_OUT, R_OL = 59, 60, 61, 62, 63, 64
R_AV = 65
N_RECV = 69


def kernel(q_ref, k_ref, v_ref, w_ref, out_ref,
           qb, kv, att, ob, wb, mst, acc, s0, s1, newb, alpb, oacc, mixb, ss, rs):
    ctx = lax.axis_index("ctx")
    tp = lax.axis_index("tp")
    x, zl, y = ctx // (NZL * NY), (ctx // NY) % NZL, ctx % NY
    zh, c = tp // 2, tp % 2

    def dev(dx=0, dzl=0, dy=0, dzh=0, dc=0):
        return ((((x + dx) % NX) * NZL + (zl + dzl) % NZL) * NY + (y + dy) % NY,
                ((zh + dzh) % NZH) * 2 + (c + dc) % 2)

    def dev_abs(xd, r):
        return ((xd * NZL + zl) * NY + y, zh * 2 + r)

    sends = []
    count = [0]

    def send(src, dst, device, recv):
        i = count[0]
        count[0] += 1
        copy = pltpu.make_async_remote_copy(
            src_ref=src, dst_ref=dst, send_sem=ss.at[i], recv_sem=rs.at[recv],
            device_id=device, device_id_type=MESH)
        copy.start()
        sends.append(copy)

    def local(src, dst, recv):
        pltpu.make_async_copy(src, dst, rs.at[recv]).start()

    def arrived(dst, recv):
        pltpu.make_async_copy(dst, dst, rs.at[recv]).wait()

    mine = pl.ds(pl.multiple_of(c * HALF, HALF), HALF)
    theirs = pl.ds(pl.multiple_of((1 - c) * HALF, HALF), HALF)
    wcols = pl.ds(pl.multiple_of(zh * FEAT, FEAT), FEAT)

    local(w_ref.at[:, wcols], wb.at[0, c], R_WL)

    def init(n, _):
        mst[n] = jnp.full((HALF, HD), -1e30, F32)
        acc[n] = jnp.zeros((HALF, 2 * HD), F32)
        return 0

    lax.fori_loop(0, NX, init, 0)

    owner = x // 2 == c
    own_cols = pl.ds(pl.multiple_of((x % 2) * HD, HD), HD)

    @pl.when(owner)
    def _():
        local(k_ref.at[mine, own_cols], kv.at[0, 0, mine, :], R_A)
        local(v_ref.at[mine, own_cols], kv.at[0, 1, mine, :], R_AV)
        local(q_ref.at[mine, own_cols], qb.at[0], R_Q)

    peers = [dev(dx=d, dc=e) for d in (1, 2, 3) for e in (0, 1)]
    peers += [dev(dc=1), dev(dzl=1)]
    peers += [dev(dzh=d) for d in (1, 2, 3)]
    barrier = pltpu.get_barrier_semaphore()
    for peer in peers:
        pl.semaphore_signal(barrier, inc=1, device_id=peer, device_id_type=MESH)
    pl.semaphore_wait(barrier, len(peers))

    def descriptor(src, dst, device, recv):
        i = count[0]
        count[0] += 1
        copy = pltpu.make_async_remote_copy(
            src_ref=src, dst_ref=dst, send_sem=ss.at[i], recv_sem=rs.at[recv],
            device_id=device, device_id_type=MESH)
        sends.append(copy)
        return copy

    def pass_own(d, n):
        piece = kv.at[d, n, mine, :]
        return [descriptor(piece, kv.at[4 + d, n, mine, :], dev(dzl=1), R_Z + d),
                descriptor(piece, piece, dev(dc=1), R_B + d)]

    own = pass_own(0, 0) + pass_own(0, 1)

    def start_own():
        arrived(kv.at[0, 0, mine, :], R_A)
        arrived(kv.at[0, 1, mine, :], R_AV)
        for copy in own:
            copy.start()

    @pl.when(owner)
    def _():
        start_own()

    wrow = pl.ds(pl.multiple_of((x % 2) * HD, HD), HD)
    wcol = (x // 2) * FC
    wslice = wb.at[pl.ds(1, 3), c, wrow, pl.ds(pl.multiple_of(wcol, FC), FC)]

    def weights_z():
        for d in (1, 3, 2):
            zd = (zh + d) % NZH
            send(w_ref.at[wrow, pl.ds(pl.multiple_of(zd * FEAT + wcol, FC), FC)],
                 wb.at[4 - d, c, wrow, pl.ds(pl.multiple_of(wcol, FC), FC)],
                 dev(dzh=d), R_WZ + 4 - d)

    def weights_x():
        for d in (1, 2, 3):
            arrived(wb.at[d, c, wrow, pl.ds(pl.multiple_of(wcol, FC), FC)], R_WZ + d)
        for d in (1, 3, 2):
            send(wslice, wslice, dev(dx=d), R_WX + d)

    def weights_core():
        for d in (1, 2, 3):
            arrived(wslice, R_WX + d)
        send(wb.at[pl.ds(1, 3), c], wb.at[pl.ds(1, 3), c], dev(dc=1), R_WP)

    first = jnp.where((2 * c - x) % NX == 2, 1, 0)
    waits = []

    def exchange(j, when):
        head = (j + first) % 2
        xd = 2 * c + head
        slot = (x - xd) % NX
        cols = pl.ds(pl.multiple_of(head * HD, HD), HD)
        for src, dst, recv in ((k_ref, kv.at[slot, 0], R_A), (v_ref, kv.at[slot, 1], R_AV),
                               (q_ref, qb.at[slot], R_Q)):
            for r in (0, 1):
                rows = pl.ds(r * HALF, HALF)
                i = count[0]
                count[0] += 1
                copy = pltpu.make_async_remote_copy(
                    src_ref=src.at[rows, cols], dst_ref=dst if recv == R_Q else dst.at[rows, :],
                    send_sem=ss.at[i], recv_sem=rs.at[recv + slot],
                    device_id=dev_abs(xd, r), device_id_type=MESH)
                go = jnp.logical_not((xd == x) & (c == r)) & when

                @pl.when(go)
                def _():
                    copy.start()

                def drain(copy=copy, go=go):
                    @pl.when(go)
                    def _():
                        copy.wait_send()

                waits.append(drain)

    always = c >= 0
    exchange(0, always)
    exchange(1, always)

    tq = HALF // 2

    def scores(i, s, buf):
        k = kv[s, 0]
        for rows in (pl.ds(0, HALF),):
            sc = lax.dot_general(qb[i, rows, :], k, (((1,), (1,)), ((), ())),
                                 preferred_element_type=F32)
            (s0, s1)[buf][rows, :] = sc
            old = mst[i, rows, :]
            new = jnp.maximum(old, jnp.max(sc, axis=1, keepdims=True) * SCALE)
            mst[i, rows, :] = new
            newb[buf, rows, :] = new
            alpb[buf, rows, :] = jnp.exp2(old - new)

    def absorb(i, s, buf):
        v = jnp.concatenate([kv[s, 1], jnp.ones((TOK, HD), BF)], axis=1)
        for t in range(HALF // tq):
            rows = pl.ds(t * tq, tq)
            new = newb[buf, rows, :]
            alpha = alpb[buf, rows, :]
            p = jnp.exp2((s0, s1)[buf][rows, :] * SCALE
                         - jnp.concatenate([new] * (TOK // HD), axis=1)).astype(BF)
            pv = jnp.dot(p, v, preferred_element_type=F32)
            acc[i, rows, :] = acc[i, rows, :] * jnp.concatenate([alpha, alpha], axis=1) + pv

    pending = []

    def step(i, s):
        buf = len(pending) % 2
        scores(i, s, buf)
        if pending:
            absorb(*pending[-1], 1 - buf)
        pending.append((i, s))

    def items(pairs):
        for i, n in pairs:
            step(i, n)

    def half_of(s, rows):
        return kv.at[s, :, rows, :]

    def pass_on(d, n):
        arrived(kv.at[d, n, mine, :], (R_A, R_AV)[n] + d)
        for copy in pass_own(d, n):
            copy.start()

    def pass_other(d):
        arrived(half_of(4 + d, mine), R_Z + d)
        send(half_of(4 + d, mine), half_of(4 + d, mine), dev(dc=1), R_B + 4 + d)

    def whole(s):
        arrived(half_of(s, theirs), R_B + s)

    def queries(d):
        arrived(qb.at[d], R_Q + d)

    @pl.when(jnp.logical_not(owner))
    def _():
        start_own()

    send(w_ref.at[:, wcols], wb.at[0, c], dev(dc=1), R_WO)
    queries(0)
    whole(0)
    step(0, 0)
    pass_on(1, 0)
    pass_on(3, 0)
    pass_on(1, 1)
    pass_on(3, 1)
    pass_other(0)
    whole(1)
    whole(3)
    items([(0, 1), (0, 3)])
    whole(4)
    queries(1)
    queries(3)
    items([(0, 4), (1, 0), (1, 1), (1, 3), (1, 4), (3, 0)])
    pass_other(1)
    items([(3, 1)])
    pass_on(2, 0)
    pass_on(2, 1)
    items([(3, 3), (3, 4)])
    whole(5)
    items([(0, 5), (1, 5), (3, 5)])
    whole(2)
    items([(0, 2), (1, 2)])
    queries(2)
    pass_other(3)
    items([(3, 2), (2, 0), (2, 1)])
    weights_z()
    items([(2, 3), (2, 4), (2, 5)])
    whole(7)
    items([(2, 2), (0, 7)])
    pass_other(2)
    items([(1, 7), (3, 7)])
    step(2, 7)
    whole(6)

    def finish(i):
        ob[i] = (acc[i, :, :HD] / acc[i, :, HD:]).astype(BF)

    def give(i):
        if i == 0:
            send(ob.at[0], att.at[3, 0], dev(dzh=1), R_G3 + 0)
            send(ob.at[0], att.at[1, 0], dev(dzh=3), R_G1 + 0)
        else:
            send(ob.at[i], att.at[0, 4 - i], dev(dx=i), R_RET + 4 - i)

    step(0, 6)
    step(1, 6)
    finish(0)
    step(3, 6)
    finish(1)
    give(0)
    step(2, 6)
    finish(3)
    give(1)
    absorb(*pending[-1], (len(pending) - 1) % 2)
    finish(2)
    give(3)
    att[0, 0] = ob[0]
    give(2)

    ORDER = (0, 3, 1, 2)
    for u in ORDER[1:]:
        arrived(att.at[0, u], R_RET + u)
        send(att.at[0, u], att.at[3, u], dev(dzh=1), R_G3 + u)
        send(att.at[0, u], att.at[1, u], dev(dzh=3), R_G1 + u)
        if u == 3:
            weights_x()

    def wrows(d, u):
        head = (x + u) % NX
        return wb[d, head // 2, pl.ds(pl.multiple_of((head % 2) * HD, HD), HD), :]

    def project(pairs, start=False):
        a = jnp.concatenate([att[d, u] for d, u in pairs], axis=1)
        w = jnp.concatenate([wrows(d, u) for d, u in pairs], axis=0)
        r = jnp.dot(a, w, preferred_element_type=F32)
        oacc[...] = r if start else oacc[...] + r

    arrived(wb.at[0, c], R_WL)
    arrived(wb.at[0, 1 - c], R_WO)
    project([(0, 0), (0, 1), (0, 2), (0, 3)], True)

    lo, hi = pl.ds(0, HALF // 2), pl.ds(HALF // 2, HALF // 2)

    def relay(u):
        arrived(att.at[3, u], R_G3 + u)
        send(att.at[3, u, lo, :], att.at[2, u, lo, :], dev(dzh=1), R_H + u)
        arrived(att.at[1, u], R_G1 + u)
        send(att.at[1, u, hi, :], att.at[2, u, hi, :], dev(dzh=3), R_H + 4 + u)

    relay(0)
    relay(3)
    relay(1)
    relay(2)
    weights_core()
    arrived(wb.at[pl.ds(1, 3), 1 - c], R_WP)
    project([(3, 0), (3, 1), (3, 2), (3, 3)])
    project([(1, 0), (1, 1), (1, 2), (1, 3)])

    def last(us):
        for u in us:
            arrived(att.at[2, u, lo, :], R_H + u)
            arrived(att.at[2, u, hi, :], R_H + 4 + u)
        project([(2, u) for u in us])

    last((0, 3))
    last((1,))
    arrived(att.at[2, 2, lo, :], R_H + 2)
    arrived(att.at[2, 2, hi, :], R_H + 4 + 2)
    head = (x + 2) % NX
    for n, core in ((1, 1 - c), (0, c)):
        cols = pl.ds(pl.multiple_of(core * FC, FC), FC)
        w = wb[2, head // 2, pl.ds(pl.multiple_of((head % 2) * HD, HD), HD), cols]
        mixb[n] = (oacc[:, cols] + jnp.dot(att[2, 2], w, preferred_element_type=F32)).astype(BF)
    send(mixb.at[1], out_ref.at[mine, :], dev(dc=1), R_OUT)
    local(mixb.at[0], out_ref.at[mine, :], R_OL)
    arrived(out_ref.at[mine, :], R_OL)
    arrived(out_ref.at[theirs, :], R_OUT)

    for drain in waits:
        drain()
    for copy in sends:
        copy.wait_send()


N_SEND = 96


def body(queries, keys, values, residual, gate, out_weight):
    projected = pl.pallas_call(
        kernel,
        out_shape=pltpu.VMEM((TOK, FC), BF),
        in_specs=[pl.BlockSpec(memory_space=pltpu.HBM)] * 4,
        out_specs=pl.BlockSpec(memory_space=pltpu.VMEM),
        scratch_shapes=[
            pltpu.VMEM((NX, HALF, HD), BF),
            pltpu.VMEM((2 * NX, 2, TOK, HD), BF),
            pltpu.VMEM((NZH, NX, HALF, HD), BF),
            pltpu.VMEM((NX, HALF, HD), BF),
            pltpu.VMEM((NZH, 2, 256, FEAT), BF),
            pltpu.VMEM((NX, HALF, HD), F32),
            pltpu.VMEM((NX, HALF, 2 * HD), F32),
            pltpu.VMEM((HALF, TOK), F32),
            pltpu.VMEM((HALF, TOK), F32),
            pltpu.VMEM((2, HALF, HD), F32),
            pltpu.VMEM((2, HALF, HD), F32),
            pltpu.VMEM((HALF, FEAT), F32),
            pltpu.VMEM((2, HALF, FC), BF),
            pltpu.SemaphoreType.DMA((N_SEND,)),
            pltpu.SemaphoreType.DMA((N_RECV,)),
        ],
        compiler_params=pltpu.CompilerParams(
            collective_id=0, has_side_effects=True, vmem_limit_bytes=60 * 2**20),
        name="attention",
    )(queries, keys, values, out_weight)
    return (residual.astype(F32) + gate[None, :] * projected.astype(F32)).astype(BF)


def solution(mesh):
    return jax.shard_map(
        body,
        mesh=mesh,
        in_specs=(
            P("ctx", "tp"),
            P("ctx", "tp"),
            P("ctx", "tp"),
            P("ctx", "tp"),
            P("tp"),
            P("tp", None),
        ),
        out_specs=P("ctx", "tp"),
        check_vma=False,
    )
```
